128 devices in a mesh: cam: 4 (over z_hi, core), lmk: 32 (over y, z_lo, x).
Axes of the slice: x: 4, y: 4, z: 4 (z_hi: 2, z_lo: 2; z = z_hi * 2 + z_lo), core: 2. Of those that a mesh axis runs over, the one named last changes fastest.
Arguments:
- probes: bfloat16 [128, 32, 576], P(('cam', 'lmk')), may hold values from -6 to 6
- u_inverse: bfloat16 [128, 576, 576], P(('cam', 'lmk')), may hold values from -1 to 3
- couplings: bfloat16 [10240, 576, 192], P(('cam', 'lmk')), may hold values from -0.09375 to 0.09375
- v_inverse: bfloat16 [1536, 192, 192], P('lmk'), may hold values from -3 to 4
- tile_cam: int32 [10240], P(('cam', 'lmk')), may hold values from 0 to 31
- tile_lmk: int32 [10240], P(('cam', 'lmk')), may hold values from 0 to 47
Outputs:
- solution: float32 [128, 32, 576], P(('cam', 'lmk'))
The draws below stay inside these ranges and needn't reach their ends.
All inputs are finite; a program needn't handle non-finite values.
Results may differ from the reference program's by a relative error of at most 0.012.
Values may be sent and summed in bfloat16 or wider, within the bound.
A program may use at most 128 MiB of HBM per device.

```python
import math
import jax
import jax.numpy as jnp
from jax import lax

CP = 576
LP = 192
PROBES = 32
POWERS = 4
CAM_DEV = 1
TILE_DEV = 80
LBD = 48
CAM_GROUP = 32
NC = 128
NL = 1536
TILES = 10240
N_CAM = 4
N_LMK = 32


def dominant_blocks(diag, noise, width, factor):
    eye = jnp.eye(width, dtype=jnp.float32)
    blocks = diag[:, :, None] * eye[None, :, :] + noise * (0.3 / math.sqrt(width))
    return (factor * blocks).astype(jnp.bfloat16)


def drawn_parts(key, count, width):
    first, second = jax.random.split(key)
    diag = jax.random.uniform(first, (count, width), jnp.float32, 0.7, 1.3)
    noise = jax.random.normal(second, (count, width, width), jnp.float32)
    return (diag, noise)


def draw_u_inverse(key, part):
    own_key = jax.random.fold_in(key, 11)
    diag, noise = drawn_parts(own_key, NC, CP)
    return dominant_blocks(diag, noise, CP, 1.0)


def draw_v_inverse(key, part):
    own_key = jax.random.fold_in(key, 23)
    factor = 0.6 * math.sqrt(CAM_DEV * CP * N_CAM / (LP * LBD))
    diag, noise = drawn_parts(own_key, NL, LP)
    return dominant_blocks(diag, noise, LP, factor)


def place_ends(drawn, key, smallest, high):
    place = [jax.random.randint(jax.random.fold_in(key, axis), (), 0, length) for axis, length in enumerate(drawn.shape)]
    main_axis = drawn.shape.index(max(drawn.shape))
    neighbour = place[:main_axis] + [(place[main_axis] + 1) % drawn.shape[main_axis]] + place[main_axis + 1:]
    return drawn.at[tuple(place)].set(smallest).at[tuple(neighbour)].set(high)


def block_levels(rng, shape, cuts, smallest, largest):
    gain = 1.0
    for dim, shards_of in cuts:
        heights = jax.random.uniform(jax.random.fold_in(jax.random.fold_in(rng, 6), dim), (shards_of,), jnp.float32, smallest / len(cuts), largest / len(cuts))
        gain = gain * jnp.repeat(jnp.exp(heights), shape[dim] // shards_of).reshape((-1,) + (1,) * (len(shape) - 1 - dim))
    return gain


def normal_values(key, dims, scale, reach, shards=(), kind=jnp.bfloat16):
    result = scale * jax.random.normal(key, dims, jnp.float32)
    if shards:
        result = result * block_levels(key, dims, shards, -0.22, 0.18)
    return jnp.clip(result, -reach, reach).astype(kind)


def setup_inputs(seed: int = 0) -> dict:
    key_list = jax.random.split(jax.random.key(seed), 7)
    return {
        "probes": normal_values(key_list[0], (NC, PROBES, CP), 1.0, 6.0, ((0, 128),)),
        "u_inverse": draw_u_inverse(jax.random.fold_in(key_list[6], 71), 0),
        "couplings": normal_values(key_list[2], (TILES, CP, LP), (CP * N_CAM * TILE_DEV // LBD) ** -0.5, 0.09375, ((0, 128),)),
        "v_inverse": draw_v_inverse(jax.random.fold_in(key_list[6], 71), 0),
        "tile_cam": place_ends(jax.random.randint(key_list[4], (TILES,), 0, CAM_GROUP), jax.random.fold_in(key_list[4], 1), 0, CAM_GROUP - 1).astype(jnp.int32),
        "tile_lmk": place_ends(jax.random.randint(key_list[5], (TILES,), 0, LBD), jax.random.fold_in(key_list[5], 1), 0, LBD - 1).astype(jnp.int32),
    }


def reference(probes, u_inverse, couplings, v_inverse, tile_cam, tile_lmk):
    u_full = u_inverse.astype(jnp.float32)
    v_full = v_inverse.astype(jnp.float32)
    current = jnp.einsum('bpc,bcd->bpd', probes.astype(jnp.float32), u_full)
    solution = current
    devices = N_CAM * N_LMK
    for power_step in range(POWERS):
        panel = lax.optimization_barrier(current.astype(jnp.bfloat16)).astype(jnp.float32)

        def forward_step(landmark_sum, device):
            group_idx = (device // N_LMK).astype(jnp.int32)
            shard_idx = (device % N_LMK).astype(jnp.int32)
            start = (device * TILE_DEV).astype(jnp.int32)
            tiles = lax.dynamic_slice_in_dim(couplings, start, TILE_DEV, 0).astype(jnp.float32)
            cams = group_idx * CAM_GROUP + lax.dynamic_slice_in_dim(tile_cam, start, TILE_DEV, 0)
            lmks = shard_idx * LBD + lax.dynamic_slice_in_dim(tile_lmk, start, TILE_DEV, 0)
            contrib = jnp.einsum('tpc,tcl->tpl', panel[cams], tiles)
            return landmark_sum.at[lmks].add(contrib), None

        landmark_sum, _ = lax.scan(forward_step, jnp.zeros((NL, PROBES, LP), jnp.float32), jnp.arange(devices, dtype=jnp.int32))
        rounded = lax.optimization_barrier(landmark_sum.astype(jnp.bfloat16)).astype(jnp.float32)
        applied = jnp.einsum('mpl,mlq->mpq', rounded, v_full).astype(jnp.bfloat16).astype(jnp.float32)

        def backward_step(camera_sum, device):
            group_idx = (device // N_LMK).astype(jnp.int32)
            shard_idx = (device % N_LMK).astype(jnp.int32)
            start = (device * TILE_DEV).astype(jnp.int32)
            tiles = lax.dynamic_slice_in_dim(couplings, start, TILE_DEV, 0).astype(jnp.float32)
            cams = group_idx * CAM_GROUP + lax.dynamic_slice_in_dim(tile_cam, start, TILE_DEV, 0)
            lmks = shard_idx * LBD + lax.dynamic_slice_in_dim(tile_lmk, start, TILE_DEV, 0)
            contrib = jnp.einsum('tpl,tcl->tpc', applied[lmks], tiles)
            return camera_sum.at[cams].add(contrib), None

        camera_sum, _ = lax.scan(backward_step, jnp.zeros((NC, PROBES, CP), jnp.float32), jnp.arange(devices, dtype=jnp.int32))
        rounded_cam = lax.optimization_barrier(camera_sum.astype(jnp.bfloat16)).astype(jnp.float32)
        current = jnp.einsum('bpc,bcd->bpd', rounded_cam, u_full)
        solution = solution + current
    return solution
```

```python
import jax
import jax.numpy as jnp
from jax import lax
from jax.sharding import PartitionSpec as P

POWERS = 4


def onehot_sum(selected, values):
    upper = values.astype(jnp.bfloat16)
    lower = (values - upper.astype(jnp.float32)).astype(jnp.bfloat16)
    first = jnp.einsum("st,tpx->spx", selected, upper, preferred_element_type=jnp.float32)
    second = jnp.einsum("st,tpx->spx", selected, lower, preferred_element_type=jnp.float32)
    return first + second


def a2a_gather(block, axis_name):
    size = lax.axis_size(axis_name)
    tiled = jnp.broadcast_to(block[None], (size,) + block.shape)
    got = lax.all_to_all(tiled, axis_name, 0, 0, tiled=False)
    return got.reshape((size * block.shape[0],) + block.shape[1:])


def a2a_reduce_scatter(full, axis_name):
    size = lax.axis_size(axis_name)
    chunks = full.reshape((size, full.shape[0] // size) + full.shape[1:])
    got = lax.all_to_all(chunks, axis_name, 0, 0, tiled=False)
    return jnp.sum(got, axis=0)


def a2a_allreduce(full, axis_name):
    size = lax.axis_size(axis_name)
    tiled = jnp.broadcast_to(full[None], (size,) + full.shape)
    got = lax.all_to_all(tiled, axis_name, 0, 0, tiled=False)
    return jnp.sum(got, axis=0)


def local(probes, u_inverse, couplings, v_inverse, tile_cam, tile_lmk):
    group_size = lax.axis_size("lmk") * u_inverse.shape[0]
    landmark_count = v_inverse.shape[0]
    cam_onehot = (tile_cam[None, :] == jnp.arange(group_size, dtype=jnp.int32)[:, None]).astype(
        jnp.bfloat16
    )
    lmk_onehot = (tile_lmk[None, :] == jnp.arange(landmark_count, dtype=jnp.int32)[:, None]).astype(
        jnp.bfloat16
    )
    current = jnp.einsum("bpc,bcd->bpd", probes, u_inverse, preferred_element_type=jnp.float32)
    series_sum = current
    panel = a2a_gather(current.astype(jnp.bfloat16), "lmk")
    for power_step in range(POWERS):
        tile_rows = jnp.take(panel, tile_cam, axis=0)
        forward = jnp.einsum(
            "tpc,tcl->tpl", tile_rows, couplings, preferred_element_type=jnp.float32
        )
        partial_value = onehot_sum(lmk_onehot, forward)
        landmark_sum = a2a_allreduce(partial_value, "cam")
        landmark_out = jnp.einsum(
            "mpl,mlq->mpq",
            landmark_sum.astype(jnp.bfloat16),
            v_inverse,
            preferred_element_type=jnp.float32,
        ).astype(jnp.bfloat16)
        picked = jnp.take(landmark_out, tile_lmk, axis=0)
        backward = jnp.einsum("tpl,tcl->tpc", picked, couplings, preferred_element_type=jnp.float32)
        camera_sum = a2a_reduce_scatter(onehot_sum(cam_onehot, backward), "lmk")
        current = jnp.einsum(
            "bpc,bcd->bpd",
            camera_sum.astype(jnp.bfloat16),
            u_inverse,
            preferred_element_type=jnp.float32,
        )
        series_sum = series_sum + current
        if power_step + 1 < POWERS:
            panel = a2a_gather(current.astype(jnp.bfloat16), "lmk")
    return series_sum


def solution(mesh):
    in_specs = (
        P(("cam", "lmk"), None, None),
        P(("cam", "lmk"), None, None),
        P(("cam", "lmk"), None, None),
        P("lmk", None, None),
        P(("cam", "lmk")),
        P(("cam", "lmk")),
    )
    out_specs = P(("cam", "lmk"), None, None)
    return jax.shard_map(local, mesh=mesh, in_specs=in_specs, out_specs=out_specs, check_vma=False)
```

```python
import jax
import jax.numpy as jnp
from jax import lax
from jax.sharding import PartitionSpec as P

POWERS = 4


def onehot_sum(selected, values):
    upper = values.astype(jnp.bfloat16)
    lower = (values - upper.astype(jnp.float32)).astype(jnp.bfloat16)
    first = jnp.einsum("st,tpx->spx", selected, upper, preferred_element_type=jnp.float32)
    second = jnp.einsum("st,tpx->spx", selected, lower, preferred_element_type=jnp.float32)
    return first + second


def a2a_gather(block, axis_name):
    size = lax.axis_size(axis_name)
    tiled = jnp.broadcast_to(block[None], (size,) + block.shape)
    got = lax.all_to_all(tiled, axis_name, 0, 0, tiled=False)
    return got.reshape((size * block.shape[0],) + block.shape[1:])


def a2a_reduce_scatter(full, axis_name):
    size = lax.axis_size(axis_name)
    chunks = full.reshape((size, full.shape[0] // size) + full.shape[1:])
    got = lax.all_to_all(chunks, axis_name, 0, 0, tiled=False)
    return jnp.sum(got, axis=0)


def a2a_allreduce(full, axis_name):
    size = lax.axis_size(axis_name)
    tiled = jnp.broadcast_to(full[None], (size,) + full.shape)
    got = lax.all_to_all(tiled, axis_name, 0, 0, tiled=False)
    return jnp.sum(got, axis=0)


def local(probes, u_inverse, couplings, v_inverse, tile_cam, tile_lmk):
    group_size = lax.axis_size("lmk") * u_inverse.shape[0]
    landmark_count = v_inverse.shape[0]
    cam_onehot = (tile_cam[None, :] == jnp.arange(group_size, dtype=jnp.int32)[:, None]).astype(
        jnp.bfloat16
    )
    lmk_onehot = (tile_lmk[None, :] == jnp.arange(landmark_count, dtype=jnp.int32)[:, None]).astype(
        jnp.bfloat16
    )
    cam_count = lax.axis_size("cam")
    part_size = landmark_count // cam_count
    v_part = lax.dynamic_slice_in_dim(v_inverse, lax.axis_index("cam") * part_size, part_size, 0)
    current = jnp.einsum("bpc,bcd->bpd", probes, u_inverse, preferred_element_type=jnp.float32)
    series_sum = current
    panel = a2a_gather(current.astype(jnp.bfloat16), "lmk")
    for power_step in range(POWERS):
        tile_rows = jnp.take(panel, tile_cam, axis=0)
        forward = jnp.einsum(
            "tpc,tcl->tpl", tile_rows, couplings, preferred_element_type=jnp.float32
        )
        partial_value = onehot_sum(lmk_onehot, forward)
        landmark_part = a2a_reduce_scatter(partial_value, "cam")
        landmark_part_out = jnp.einsum(
            "mpl,mlq->mpq",
            landmark_part.astype(jnp.bfloat16),
            v_part,
            preferred_element_type=jnp.float32,
        ).astype(jnp.bfloat16)
        landmark_out = a2a_gather(landmark_part_out, "cam")
        picked = jnp.take(landmark_out, tile_lmk, axis=0)
        backward = jnp.einsum("tpl,tcl->tpc", picked, couplings, preferred_element_type=jnp.float32)
        camera_sum = a2a_reduce_scatter(onehot_sum(cam_onehot, backward), "lmk")
        current = jnp.einsum(
            "bpc,bcd->bpd",
            camera_sum.astype(jnp.bfloat16),
            u_inverse,
            preferred_element_type=jnp.float32,
        )
        series_sum = series_sum + current
        if power_step + 1 < POWERS:
            panel = a2a_gather(current.astype(jnp.bfloat16), "lmk")
    return series_sum


def solution(mesh):
    in_specs = (
        P(("cam", "lmk"), None, None),
        P(("cam", "lmk"), None, None),
        P(("cam", "lmk"), None, None),
        P("lmk", None, None),
        P(("cam", "lmk")),
        P(("cam", "lmk")),
    )
    out_specs = P(("cam", "lmk"), None, None)
    return jax.shard_map(local, mesh=mesh, in_specs=in_specs, out_specs=out_specs, check_vma=False)
```

```python
import jax
import jax.numpy as jnp
from jax import lax
from jax.sharding import PartitionSpec as P

POWERS = 4


def onehot_sum(selected, values):
    upper = values.astype(jnp.bfloat16)
    lower = (values - upper.astype(jnp.float32)).astype(jnp.bfloat16)
    first = jnp.einsum("st,tpx->spx", selected, upper, preferred_element_type=jnp.float32)
    second = jnp.einsum("st,tpx->spx", selected, lower, preferred_element_type=jnp.float32)
    return first + second


def a2a_gather(block, axis_name):
    size = lax.axis_size(axis_name)
    tiled = jnp.broadcast_to(block[None], (size,) + block.shape)
    got = lax.all_to_all(tiled, axis_name, 0, 0, tiled=False)
    return got.reshape((size * block.shape[0],) + block.shape[1:])


def a2a_reduce_scatter(full, axis_name):
    size = lax.axis_size(axis_name)
    chunks = full.reshape((size, full.shape[0] // size) + full.shape[1:])
    got = lax.all_to_all(chunks.astype(jnp.bfloat16), axis_name, 0, 0, tiled=False)
    return jnp.sum(got.astype(jnp.float32), axis=0)


def a2a_allreduce(full, axis_name):
    size = lax.axis_size(axis_name)
    tiled = jnp.broadcast_to(full[None], (size,) + full.shape)
    got = lax.all_to_all(tiled, axis_name, 0, 0, tiled=False)
    return jnp.sum(got, axis=0)


def local(probes, u_inverse, couplings, v_inverse, tile_cam, tile_lmk):
    group_size = lax.axis_size("lmk") * u_inverse.shape[0]
    landmark_count = v_inverse.shape[0]
    cam_onehot = (tile_cam[None, :] == jnp.arange(group_size, dtype=jnp.int32)[:, None]).astype(
        jnp.bfloat16
    )
    lmk_onehot = (tile_lmk[None, :] == jnp.arange(landmark_count, dtype=jnp.int32)[:, None]).astype(
        jnp.bfloat16
    )
    cam_count = lax.axis_size("cam")
    part_size = landmark_count // cam_count
    v_part = lax.dynamic_slice_in_dim(v_inverse, lax.axis_index("cam") * part_size, part_size, 0)
    current = jnp.einsum("bpc,bcd->bpd", probes, u_inverse, preferred_element_type=jnp.float32)
    series_sum = current
    panel = a2a_gather(current.astype(jnp.bfloat16), "lmk")
    for power_step in range(POWERS):
        tile_rows = jnp.take(panel, tile_cam, axis=0)
        forward = jnp.einsum(
            "tpc,tcl->tpl", tile_rows, couplings, preferred_element_type=jnp.float32
        )
        partial_value = onehot_sum(lmk_onehot, forward)
        landmark_part = a2a_reduce_scatter(partial_value, "cam")
        landmark_part_out = jnp.einsum(
            "mpl,mlq->mpq",
            landmark_part.astype(jnp.bfloat16),
            v_part,
            preferred_element_type=jnp.float32,
        ).astype(jnp.bfloat16)
        landmark_out = a2a_gather(landmark_part_out, "cam")
        picked = jnp.take(landmark_out, tile_lmk, axis=0)
        backward = jnp.einsum("tpl,tcl->tpc", picked, couplings, preferred_element_type=jnp.float32)
        camera_sum = a2a_reduce_scatter(onehot_sum(cam_onehot, backward), "lmk")
        current = jnp.einsum(
            "bpc,bcd->bpd",
            camera_sum.astype(jnp.bfloat16),
            u_inverse,
            preferred_element_type=jnp.float32,
        )
        series_sum = series_sum + current
        if power_step + 1 < POWERS:
            panel = a2a_gather(current.astype(jnp.bfloat16), "lmk")
    return series_sum


def solution(mesh):
    in_specs = (
        P(("cam", "lmk"), None, None),
        P(("cam", "lmk"), None, None),
        P(("cam", "lmk"), None, None),
        P("lmk", None, None),
        P(("cam", "lmk")),
        P(("cam", "lmk")),
    )
    out_specs = P(("cam", "lmk"), None, None)
    return jax.shard_map(local, mesh=mesh, in_specs=in_specs, out_specs=out_specs, check_vma=False)
```

```python
import functools

import jax
import jax.numpy as jnp
from jax import lax
from jax.experimental import pallas as pl
from jax.experimental.pallas import tpu as pltpu
from jax.sharding import PartitionSpec as P

POWERS = 4
MESH = pl.DeviceIdType.MESH
AXES = ("cam", "lmk")
COLLECTIVE_IDS = {}


def exchange_kernel(n, axis, x_ref, o_ref, send_sem, recv_sem, local_sem):
    me = lax.axis_index(axis)
    coords = tuple(lax.axis_index(name) for name in AXES)
    slot = AXES.index(axis)

    def device(peer):
        return coords[:slot] + (peer,) + coords[slot + 1:]

    barrier = pltpu.get_barrier_semaphore()
    for step in range(1, n):
        pl.semaphore_signal(barrier, inc=1, device_id=device(lax.rem(me + step, n)), device_id_type=MESH)
    pl.semaphore_wait(barrier, n - 1)
    local = pltpu.make_async_copy(x_ref.at[me], o_ref.at[me], local_sem)
    local.start()
    sends = []
    for step in range(1, n):
        peer = lax.rem(me + step, n)
        copy = pltpu.make_async_remote_copy(
            src_ref=x_ref.at[peer],
            dst_ref=o_ref.at[me],
            send_sem=send_sem.at[step],
            recv_sem=recv_sem.at[step],
            device_id=device(peer),
            device_id_type=MESH,
        )
        copy.start()
        sends.append(copy)
    local.wait()
    for copy in sends:
        copy.wait_send()
    for step in range(1, n):
        source = lax.rem(me + n - step, n)
        pltpu.make_async_remote_copy(
            src_ref=x_ref.at[source],
            dst_ref=o_ref.at[source],
            send_sem=send_sem.at[step],
            recv_sem=recv_sem.at[step],
            device_id=device(source),
            device_id_type=MESH,
        ).wait_recv()


def exchange(x, axis_name):
    n = lax.axis_size(axis_name)
    key = (axis_name, x.shape, str(x.dtype))
    if key not in COLLECTIVE_IDS:
        COLLECTIVE_IDS[key] = len(COLLECTIVE_IDS)
    return pl.pallas_call(
        functools.partial(exchange_kernel, n, axis_name),
        out_shape=jax.ShapeDtypeStruct(x.shape, x.dtype),
        in_specs=[pl.BlockSpec(memory_space=pl.ANY)],
        out_specs=pl.BlockSpec(memory_space=pl.ANY),
        scratch_shapes=[
            pltpu.SemaphoreType.DMA((n,)),
            pltpu.SemaphoreType.DMA((n,)),
            pltpu.SemaphoreType.DMA,
        ],
        compiler_params=pltpu.CompilerParams(collective_id=COLLECTIVE_IDS[key], has_side_effects=True),
    )(x)


def onehot_sum(selected, values):
    upper = values.astype(jnp.bfloat16)
    lower = (values - upper.astype(jnp.float32)).astype(jnp.bfloat16)
    first = jnp.einsum("st,tpx->spx", selected, upper, preferred_element_type=jnp.float32)
    second = jnp.einsum("st,tpx->spx", selected, lower, preferred_element_type=jnp.float32)
    return first + second


def a2a_gather(block, axis_name):
    size = lax.axis_size(axis_name)
    tiled = jnp.broadcast_to(block[None], (size,) + block.shape)
    got = exchange(tiled, axis_name)
    return got.reshape((size * block.shape[0],) + block.shape[1:])


def a2a_reduce_scatter(full, axis_name):
    size = lax.axis_size(axis_name)
    chunks = full.reshape((size, full.shape[0] // size) + full.shape[1:])
    got = exchange(chunks.astype(jnp.bfloat16), axis_name)
    return jnp.sum(got.astype(jnp.float32), axis=0)


def a2a_allreduce(full, axis_name):
    size = lax.axis_size(axis_name)
    tiled = jnp.broadcast_to(full[None], (size,) + full.shape)
    got = exchange(tiled, axis_name)
    return jnp.sum(got, axis=0)


def local(probes, u_inverse, couplings, v_inverse, tile_cam, tile_lmk):
    group_size = lax.axis_size("lmk") * u_inverse.shape[0]
    landmark_count = v_inverse.shape[0]
    cam_onehot = (tile_cam[None, :] == jnp.arange(group_size, dtype=jnp.int32)[:, None]).astype(
        jnp.bfloat16
    )
    lmk_onehot = (tile_lmk[None, :] == jnp.arange(landmark_count, dtype=jnp.int32)[:, None]).astype(
        jnp.bfloat16
    )
    cam_count = lax.axis_size("cam")
    part_size = landmark_count // cam_count
    v_part = lax.dynamic_slice_in_dim(v_inverse, lax.axis_index("cam") * part_size, part_size, 0)
    current = jnp.einsum("bpc,bcd->bpd", probes, u_inverse, preferred_element_type=jnp.float32)
    series_sum = current
    panel = a2a_gather(current.astype(jnp.bfloat16), "lmk")
    for power_step in range(POWERS):
        tile_rows = jnp.take(panel, tile_cam, axis=0)
        forward = jnp.einsum(
            "tpc,tcl->tpl", tile_rows, couplings, preferred_element_type=jnp.float32
        )
        partial_value = onehot_sum(lmk_onehot, forward)
        landmark_part = a2a_reduce_scatter(partial_value, "cam")
        landmark_part_out = jnp.einsum(
            "mpl,mlq->mpq",
            landmark_part.astype(jnp.bfloat16),
            v_part,
            preferred_element_type=jnp.float32,
        ).astype(jnp.bfloat16)
        landmark_out = a2a_gather(landmark_part_out, "cam")
        picked = jnp.take(landmark_out, tile_lmk, axis=0)
        backward = jnp.einsum("tpl,tcl->tpc", picked, couplings, preferred_element_type=jnp.float32)
        camera_sum = a2a_reduce_scatter(onehot_sum(cam_onehot, backward), "lmk")
        current = jnp.einsum(
            "bpc,bcd->bpd",
            camera_sum.astype(jnp.bfloat16),
            u_inverse,
            preferred_element_type=jnp.float32,
        )
        series_sum = series_sum + current
        if power_step + 1 < POWERS:
            panel = a2a_gather(current.astype(jnp.bfloat16), "lmk")
    return series_sum


def solution(mesh):
    COLLECTIVE_IDS.clear()
    in_specs = (
        P(("cam", "lmk"), None, None),
        P(("cam", "lmk"), None, None),
        P(("cam", "lmk"), None, None),
        P("lmk", None, None),
        P(("cam", "lmk")),
        P(("cam", "lmk")),
    )
    out_specs = P(("cam", "lmk"), None, None)
    return jax.shard_map(local, mesh=mesh, in_specs=in_specs, out_specs=out_specs, check_vma=False)
```

```python
import functools

import jax
import jax.numpy as jnp
from jax import lax
from jax.experimental import pallas as pl
from jax.experimental.pallas import tpu as pltpu
from jax.sharding import PartitionSpec as P

POWERS = 4
MESH = pl.DeviceIdType.MESH
AXES = ("cam", "lmk")
COLLECTIVE_IDS = {}


def exchange_kernel(n, axis, gather, x_ref, o_ref, send_sem, recv_sem, local_sem):
    me = lax.axis_index(axis)
    coords = tuple(lax.axis_index(name) for name in AXES)
    slot = AXES.index(axis)

    def device(peer):
        return coords[:slot] + (peer,) + coords[slot + 1:]

    barrier = pltpu.get_barrier_semaphore()
    for step in range(1, n):
        pl.semaphore_signal(barrier, inc=1, device_id=device(lax.rem(me + step, n)), device_id_type=MESH)
    pl.semaphore_wait(barrier, n - 1)
    local = pltpu.make_async_copy(x_ref if gather else x_ref.at[me], o_ref.at[me], local_sem)
    local.start()
    sends = []
    for step in range(1, n):
        peer = lax.rem(me + step, n)
        copy = pltpu.make_async_remote_copy(
            src_ref=x_ref if gather else x_ref.at[peer],
            dst_ref=o_ref.at[me],
            send_sem=send_sem.at[step],
            recv_sem=recv_sem.at[step],
            device_id=device(peer),
            device_id_type=MESH,
        )
        copy.start()
        sends.append(copy)
    local.wait()
    for copy in sends:
        copy.wait_send()
    for step in range(1, n):
        source = lax.rem(me + n - step, n)
        pltpu.make_async_remote_copy(
            src_ref=o_ref.at[source],
            dst_ref=o_ref.at[source],
            send_sem=send_sem.at[step],
            recv_sem=recv_sem.at[step],
            device_id=device(source),
            device_id_type=MESH,
        ).wait_recv()


def exchange(x, axis_name, gather=False):
    n = lax.axis_size(axis_name)
    key = (axis_name, gather, x.shape, str(x.dtype))
    if key not in COLLECTIVE_IDS:
        COLLECTIVE_IDS[key] = len(COLLECTIVE_IDS)
    shape = (n,) + x.shape if gather else x.shape
    return pl.pallas_call(
        functools.partial(exchange_kernel, n, axis_name, gather),
        out_shape=jax.ShapeDtypeStruct(shape, x.dtype),
        in_specs=[pl.BlockSpec(memory_space=pl.ANY)],
        out_specs=pl.BlockSpec(memory_space=pl.ANY),
        scratch_shapes=[
            pltpu.SemaphoreType.DMA((n,)),
            pltpu.SemaphoreType.DMA((n,)),
            pltpu.SemaphoreType.DMA,
        ],
        compiler_params=pltpu.CompilerParams(collective_id=COLLECTIVE_IDS[key], has_side_effects=True),
    )(x)


def onehot_sum(selected, values):
    upper = values.astype(jnp.bfloat16)
    lower = (values - upper.astype(jnp.float32)).astype(jnp.bfloat16)
    first = jnp.einsum("st,tpx->spx", selected, upper, preferred_element_type=jnp.float32)
    second = jnp.einsum("st,tpx->spx", selected, lower, preferred_element_type=jnp.float32)
    return first + second


def a2a_gather(block, axis_name):
    size = lax.axis_size(axis_name)
    if axis_name == "cam":
        got = exchange(block, axis_name, gather=True)
    else:
        tiled = jnp.broadcast_to(block[None], (size,) + block.shape)
        got = lax.all_to_all(tiled, axis_name, 0, 0, tiled=False)
    return got.reshape((size * block.shape[0],) + block.shape[1:])


def a2a_reduce_scatter(full, axis_name):
    size = lax.axis_size(axis_name)
    chunks = full.reshape((size, full.shape[0] // size) + full.shape[1:])
    if axis_name == "cam":
        got = exchange(chunks.astype(jnp.bfloat16), axis_name)
    else:
        got = lax.all_to_all(chunks.astype(jnp.bfloat16), axis_name, 0, 0, tiled=False)
    return jnp.sum(got.astype(jnp.float32), axis=0)


def local(probes, u_inverse, couplings, v_inverse, tile_cam, tile_lmk):
    group_size = lax.axis_size("lmk") * u_inverse.shape[0]
    landmark_count = v_inverse.shape[0]
    cam_onehot = (tile_cam[None, :] == jnp.arange(group_size, dtype=jnp.int32)[:, None]).astype(
        jnp.bfloat16
    )
    lmk_onehot = (tile_lmk[None, :] == jnp.arange(landmark_count, dtype=jnp.int32)[:, None]).astype(
        jnp.bfloat16
    )
    cam_count = lax.axis_size("cam")
    part_size = landmark_count // cam_count
    v_part = lax.dynamic_slice_in_dim(v_inverse, lax.axis_index("cam") * part_size, part_size, 0)
    current = jnp.einsum("bpc,bcd->bpd", probes, u_inverse, preferred_element_type=jnp.float32)
    series_sum = current
    panel = a2a_gather(current.astype(jnp.bfloat16), "lmk")
    for power_step in range(POWERS):
        tile_rows = jnp.take(panel, tile_cam, axis=0)
        forward = jnp.einsum(
            "tpc,tcl->tpl", tile_rows, couplings, preferred_element_type=jnp.float32
        )
        partial_value = onehot_sum(lmk_onehot, forward)
        landmark_part = a2a_reduce_scatter(partial_value, "cam")
        landmark_part_out = jnp.einsum(
            "mpl,mlq->mpq",
            landmark_part.astype(jnp.bfloat16),
            v_part,
            preferred_element_type=jnp.float32,
        ).astype(jnp.bfloat16)
        landmark_out = a2a_gather(landmark_part_out, "cam")
        picked = jnp.take(landmark_out, tile_lmk, axis=0)
        backward = jnp.einsum("tpl,tcl->tpc", picked, couplings, preferred_element_type=jnp.float32)
        camera_sum = a2a_reduce_scatter(onehot_sum(cam_onehot, backward), "lmk")
        current = jnp.einsum(
            "bpc,bcd->bpd",
            camera_sum.astype(jnp.bfloat16),
            u_inverse,
            preferred_element_type=jnp.float32,
        )
        series_sum = series_sum + current
        if power_step + 1 < POWERS:
            panel = a2a_gather(current.astype(jnp.bfloat16), "lmk")
    return series_sum


def solution(mesh):
    COLLECTIVE_IDS.clear()
    in_specs = (
        P(("cam", "lmk"), None, None),
        P(("cam", "lmk"), None, None),
        P(("cam", "lmk"), None, None),
        P("lmk", None, None),
        P(("cam", "lmk")),
        P(("cam", "lmk")),
    )
    out_specs = P(("cam", "lmk"), None, None)
    return jax.shard_map(local, mesh=mesh, in_specs=in_specs, out_specs=out_specs, check_vma=False)
```

```python
import functools

import jax
import jax.numpy as jnp
from jax import lax
from jax.experimental import pallas as pl
from jax.experimental.pallas import tpu as pltpu
from jax.sharding import PartitionSpec as P

POWERS = 4
MESH = pl.DeviceIdType.MESH
AXES = ("cam", "lmk")
COLLECTIVE_IDS = {}


def exchange_kernel(n, axis, gather, x_ref, o_ref, send_sem, recv_sem, local_sem):
    me = lax.axis_index(axis)
    coords = tuple(lax.axis_index(name) for name in AXES)
    slot = AXES.index(axis)

    def device(peer):
        return coords[:slot] + (peer,) + coords[slot + 1:]

    barrier = pltpu.get_barrier_semaphore()
    for step in range(1, n):
        pl.semaphore_signal(barrier, inc=1, device_id=device(lax.rem(me + step, n)), device_id_type=MESH)
    pl.semaphore_wait(barrier, n - 1)
    local = pltpu.make_async_copy(x_ref if gather else x_ref.at[me], o_ref.at[me], local_sem)
    local.start()
    sends = []
    for step in range(1, n):
        peer = lax.rem(me + step, n)
        copy = pltpu.make_async_remote_copy(
            src_ref=x_ref if gather else x_ref.at[peer],
            dst_ref=o_ref.at[me],
            send_sem=send_sem.at[step],
            recv_sem=recv_sem.at[step],
            device_id=device(peer),
            device_id_type=MESH,
        )
        copy.start()
        sends.append(copy)
    local.wait()
    for copy in sends:
        copy.wait_send()
    for step in range(1, n):
        source = lax.rem(me + n - step, n)
        pltpu.make_async_remote_copy(
            src_ref=o_ref.at[source],
            dst_ref=o_ref.at[source],
            send_sem=send_sem.at[step],
            recv_sem=recv_sem.at[step],
            device_id=device(source),
            device_id_type=MESH,
        ).wait_recv()


def exchange(x, axis_name, gather=False):
    n = lax.axis_size(axis_name)
    key = (axis_name, gather, x.shape, str(x.dtype))
    if key not in COLLECTIVE_IDS:
        COLLECTIVE_IDS[key] = len(COLLECTIVE_IDS)
    shape = (n,) + x.shape if gather else x.shape
    return pl.pallas_call(
        functools.partial(exchange_kernel, n, axis_name, gather),
        out_shape=jax.ShapeDtypeStruct(shape, x.dtype),
        in_specs=[pl.BlockSpec(memory_space=pl.ANY)],
        out_specs=pl.BlockSpec(memory_space=pl.ANY),
        scratch_shapes=[
            pltpu.SemaphoreType.DMA((n,)),
            pltpu.SemaphoreType.DMA((n,)),
            pltpu.SemaphoreType.DMA,
        ],
        compiler_params=pltpu.CompilerParams(collective_id=COLLECTIVE_IDS[key], has_side_effects=True),
    )(x)


def onehot_sum(selected, values):
    upper = values.astype(jnp.bfloat16)
    lower = (values - upper.astype(jnp.float32)).astype(jnp.bfloat16)
    first = jnp.einsum("st,tpx->spx", selected, upper, preferred_element_type=jnp.float32)
    second = jnp.einsum("st,tpx->spx", selected, lower, preferred_element_type=jnp.float32)
    return first + second


def a2a_gather(block, axis_name):
    size = lax.axis_size(axis_name)
    if axis_name == "cam":
        got = exchange(block, axis_name, gather=True)
    else:
        tiled = jnp.broadcast_to(block[None], (size,) + block.shape)
        got = lax.all_to_all(tiled, axis_name, 0, 0, tiled=False)
    return got.reshape((size * block.shape[0],) + block.shape[1:])


def a2a_reduce_scatter(full, axis_name):
    size = lax.axis_size(axis_name)
    chunks = full.reshape((size, full.shape[0] // size) + full.shape[1:])
    if axis_name == "cam":
        got = exchange(chunks.astype(jnp.bfloat16), axis_name)
    else:
        got = lax.all_to_all(chunks.astype(jnp.bfloat16), axis_name, 0, 0, tiled=False)
    return jnp.sum(got.astype(jnp.float32), axis=0)


def swap_kernel(x_ref, o_ref, send_sem, recv_sem, *, partner):
    barrier = pltpu.get_barrier_semaphore()
    pl.semaphore_signal(barrier, inc=1, device_id=partner(), device_id_type=MESH)
    pl.semaphore_wait(barrier, 1)
    copy = pltpu.make_async_remote_copy(
        src_ref=x_ref,
        dst_ref=o_ref,
        send_sem=send_sem,
        recv_sem=recv_sem,
        device_id=partner(),
        device_id_type=MESH,
    )
    copy.start()
    copy.wait_send()
    copy.wait_recv()


def swap(x, flip):
    key = ("swap", flip, x.shape, str(x.dtype))
    if key not in COLLECTIVE_IDS:
        COLLECTIVE_IDS[key] = len(COLLECTIVE_IDS)

    def partner():
        return (lax.axis_index("cam") ^ flip, lax.axis_index("lmk"))

    return pl.pallas_call(
        functools.partial(swap_kernel, partner=partner),
        out_shape=jax.ShapeDtypeStruct(x.shape, x.dtype),
        in_specs=[pl.BlockSpec(memory_space=pl.ANY)],
        out_specs=pl.BlockSpec(memory_space=pl.ANY),
        scratch_shapes=[pltpu.SemaphoreType.DMA, pltpu.SemaphoreType.DMA],
        compiler_params=pltpu.CompilerParams(collective_id=COLLECTIVE_IDS[key], has_side_effects=True),
    )(x)


def pick(flag, a, b):
    return jnp.where(flag == 0, a, b)


def cam_reduce(partial_value):
    cam = lax.axis_index("cam")
    core, high = cam % 2, cam // 2
    chunks = partial_value.reshape((2, 2, partial_value.shape[0] // 4) + partial_value.shape[1:])
    mine = pick(core, chunks[:, 0], chunks[:, 1])
    theirs = pick(core, chunks[:, 1], chunks[:, 0])
    chip = mine + swap(theirs.astype(jnp.bfloat16), 1).astype(jnp.float32)
    keep = pick(high, chip[0], chip[1])
    send = pick(high, chip[1], chip[0])
    return keep + swap(send.astype(jnp.bfloat16), 2).astype(jnp.float32)


def cam_gather(block):
    cam = lax.axis_index("cam")
    core, high = cam % 2, cam // 2
    other = swap(block, 2)
    pair = pick(high, jnp.stack([block, other]), jnp.stack([other, block]))
    other_pair = swap(pair, 1)
    full = pick(core, jnp.stack([pair, other_pair], axis=1), jnp.stack([other_pair, pair], axis=1))
    return full.reshape((4 * block.shape[0],) + block.shape[1:])


def local(probes, u_inverse, couplings, v_inverse, tile_cam, tile_lmk):
    group_size = lax.axis_size("lmk") * u_inverse.shape[0]
    landmark_count = v_inverse.shape[0]
    cam_onehot = (tile_cam[None, :] == jnp.arange(group_size, dtype=jnp.int32)[:, None]).astype(
        jnp.bfloat16
    )
    lmk_onehot = (tile_lmk[None, :] == jnp.arange(landmark_count, dtype=jnp.int32)[:, None]).astype(
        jnp.bfloat16
    )
    cam_count = lax.axis_size("cam")
    part_size = landmark_count // cam_count
    v_part = lax.dynamic_slice_in_dim(v_inverse, lax.axis_index("cam") * part_size, part_size, 0)
    current = jnp.einsum("bpc,bcd->bpd", probes, u_inverse, preferred_element_type=jnp.float32)
    series_sum = current
    panel = a2a_gather(current.astype(jnp.bfloat16), "lmk")
    for power_step in range(POWERS):
        tile_rows = jnp.take(panel, tile_cam, axis=0)
        forward = jnp.einsum(
            "tpc,tcl->tpl", tile_rows, couplings, preferred_element_type=jnp.float32
        )
        partial_value = onehot_sum(lmk_onehot, forward)
        landmark_part = cam_reduce(partial_value)
        landmark_part_out = jnp.einsum(
            "mpl,mlq->mpq",
            landmark_part.astype(jnp.bfloat16),
            v_part,
            preferred_element_type=jnp.float32,
        ).astype(jnp.bfloat16)
        landmark_out = cam_gather(landmark_part_out)
        picked = jnp.take(landmark_out, tile_lmk, axis=0)
        backward = jnp.einsum("tpl,tcl->tpc", picked, couplings, preferred_element_type=jnp.float32)
        camera_sum = a2a_reduce_scatter(onehot_sum(cam_onehot, backward), "lmk")
        current = jnp.einsum(
            "bpc,bcd->bpd",
            camera_sum.astype(jnp.bfloat16),
            u_inverse,
            preferred_element_type=jnp.float32,
        )
        series_sum = series_sum + current
        if power_step + 1 < POWERS:
            panel = a2a_gather(current.astype(jnp.bfloat16), "lmk")
    return series_sum


def solution(mesh):
    COLLECTIVE_IDS.clear()
    in_specs = (
        P(("cam", "lmk"), None, None),
        P(("cam", "lmk"), None, None),
        P(("cam", "lmk"), None, None),
        P("lmk", None, None),
        P(("cam", "lmk")),
        P(("cam", "lmk")),
    )
    out_specs = P(("cam", "lmk"), None, None)
    return jax.shard_map(local, mesh=mesh, in_specs=in_specs, out_specs=out_specs, check_vma=False)
```

```python
import functools

import jax
import jax.numpy as jnp
from jax import lax
from jax.experimental import pallas as pl
from jax.experimental.pallas import tpu as pltpu
from jax.sharding import PartitionSpec as P

POWERS = 4
MESH = pl.DeviceIdType.MESH
AXES = ("cam", "lmk")
COLLECTIVE_IDS = {}


def exchange_kernel(n, axis, gather, x_ref, o_ref, send_sem, recv_sem, local_sem):
    me = lax.axis_index(axis)
    coords = tuple(lax.axis_index(name) for name in AXES)
    slot = AXES.index(axis)

    def device(peer):
        return coords[:slot] + (peer,) + coords[slot + 1:]

    barrier = pltpu.get_barrier_semaphore()
    for step in range(1, n):
        pl.semaphore_signal(barrier, inc=1, device_id=device(lax.rem(me + step, n)), device_id_type=MESH)
    pl.semaphore_wait(barrier, n - 1)
    local = pltpu.make_async_copy(x_ref if gather else x_ref.at[me], o_ref.at[me], local_sem)
    local.start()
    sends = []
    for step in range(1, n):
        peer = lax.rem(me + step, n)
        copy = pltpu.make_async_remote_copy(
            src_ref=x_ref if gather else x_ref.at[peer],
            dst_ref=o_ref.at[me],
            send_sem=send_sem.at[step],
            recv_sem=recv_sem.at[step],
            device_id=device(peer),
            device_id_type=MESH,
        )
        copy.start()
        sends.append(copy)
    local.wait()
    for copy in sends:
        copy.wait_send()
    for step in range(1, n):
        source = lax.rem(me + n - step, n)
        pltpu.make_async_remote_copy(
            src_ref=o_ref.at[source],
            dst_ref=o_ref.at[source],
            send_sem=send_sem.at[step],
            recv_sem=recv_sem.at[step],
            device_id=device(source),
            device_id_type=MESH,
        ).wait_recv()


def exchange(x, axis_name, gather=False):
    n = lax.axis_size(axis_name)
    key = (axis_name, gather, x.shape, str(x.dtype))
    if key not in COLLECTIVE_IDS:
        COLLECTIVE_IDS[key] = len(COLLECTIVE_IDS)
    shape = (n,) + x.shape if gather else x.shape
    return pl.pallas_call(
        functools.partial(exchange_kernel, n, axis_name, gather),
        out_shape=jax.ShapeDtypeStruct(shape, x.dtype),
        in_specs=[pl.BlockSpec(memory_space=pl.ANY)],
        out_specs=pl.BlockSpec(memory_space=pl.ANY),
        scratch_shapes=[
            pltpu.SemaphoreType.DMA((n,)),
            pltpu.SemaphoreType.DMA((n,)),
            pltpu.SemaphoreType.DMA,
        ],
        compiler_params=pltpu.CompilerParams(collective_id=COLLECTIVE_IDS[key], has_side_effects=True),
    )(x)


def onehot_sum(selected, values):
    upper = values.astype(jnp.bfloat16)
    lower = (values - upper.astype(jnp.float32)).astype(jnp.bfloat16)
    first = jnp.einsum("st,tpx->spx", selected, upper, preferred_element_type=jnp.float32)
    second = jnp.einsum("st,tpx->spx", selected, lower, preferred_element_type=jnp.float32)
    return first + second


def a2a_gather(block, axis_name):
    size = lax.axis_size(axis_name)
    if axis_name == "cam":
        got = exchange(block, axis_name, gather=True)
    else:
        tiled = jnp.broadcast_to(block[None], (size,) + block.shape)
        got = lax.all_to_all(tiled, axis_name, 0, 0, tiled=False)
    return got.reshape((size * block.shape[0],) + block.shape[1:])


def a2a_reduce_scatter(full, axis_name):
    size = lax.axis_size(axis_name)
    chunks = full.reshape((size, full.shape[0] // size) + full.shape[1:])
    if axis_name == "cam":
        got = exchange(chunks.astype(jnp.bfloat16), axis_name)
    else:
        got = lax.all_to_all(chunks.astype(jnp.bfloat16), axis_name, 0, 0, tiled=False)
    return jnp.sum(got.astype(jnp.float32), axis=0)


def swap_kernel(x_ref, o_ref, send_sem, recv_sem, *, partner):
    barrier = pltpu.get_barrier_semaphore()
    pl.semaphore_signal(barrier, inc=1, device_id=partner(), device_id_type=MESH)
    pl.semaphore_wait(barrier, 1)
    copy = pltpu.make_async_remote_copy(
        src_ref=x_ref,
        dst_ref=o_ref,
        send_sem=send_sem,
        recv_sem=recv_sem,
        device_id=partner(),
        device_id_type=MESH,
    )
    copy.start()
    copy.wait_send()
    copy.wait_recv()


def swap(x, flip):
    key = ("swap", flip, x.shape, str(x.dtype))
    if key not in COLLECTIVE_IDS:
        COLLECTIVE_IDS[key] = len(COLLECTIVE_IDS)

    def partner():
        return (lax.axis_index("cam") ^ flip, lax.axis_index("lmk"))

    return pl.pallas_call(
        functools.partial(swap_kernel, partner=partner),
        out_shape=jax.ShapeDtypeStruct(x.shape, x.dtype),
        in_specs=[pl.BlockSpec(memory_space=pl.ANY)],
        out_specs=pl.BlockSpec(memory_space=pl.ANY),
        scratch_shapes=[pltpu.SemaphoreType.DMA, pltpu.SemaphoreType.DMA],
        compiler_params=pltpu.CompilerParams(collective_id=COLLECTIVE_IDS[key], has_side_effects=True),
    )(x)


def take(stack, index, axis):
    return lax.dynamic_index_in_dim(stack, index, axis=axis, keepdims=False)


def cam_reduce(partial_value):
    cam = lax.axis_index("cam")
    core, high = cam % 2, cam // 2
    chunks = partial_value.reshape((2, 2, partial_value.shape[0] // 4) + partial_value.shape[1:])
    mine = take(chunks, core, 1)
    theirs = take(chunks, 1 - core, 1)
    chip = mine + swap(theirs.astype(jnp.bfloat16), 1).astype(jnp.float32)
    keep = take(chip, high, 0)
    send = take(chip, 1 - high, 0)
    return keep + swap(send.astype(jnp.bfloat16), 2).astype(jnp.float32)


def place(block, other, index, axis):
    both = jnp.stack([other, other], axis=axis)
    starts = [0] * both.ndim
    starts[axis] = index
    return lax.dynamic_update_slice(both, jnp.expand_dims(block, axis), starts)


def cam_gather(block):
    cam = lax.axis_index("cam")
    core, high = cam % 2, cam // 2
    other = swap(block, 2)
    pair = place(block, other, high, 0)
    other_pair = swap(pair, 1)
    full = place(pair, other_pair, core, 1)
    return full.reshape((4 * block.shape[0],) + block.shape[1:])


def local(probes, u_inverse, couplings, v_inverse, tile_cam, tile_lmk):
    group_size = lax.axis_size("lmk") * u_inverse.shape[0]
    landmark_count = v_inverse.shape[0]
    cam_onehot = (tile_cam[None, :] == jnp.arange(group_size, dtype=jnp.int32)[:, None]).astype(
        jnp.bfloat16
    )
    lmk_onehot = (tile_lmk[None, :] == jnp.arange(landmark_count, dtype=jnp.int32)[:, None]).astype(
        jnp.bfloat16
    )
    cam_count = lax.axis_size("cam")
    part_size = landmark_count // cam_count
    v_part = lax.dynamic_slice_in_dim(v_inverse, lax.axis_index("cam") * part_size, part_size, 0)
    current = jnp.einsum("bpc,bcd->bpd", probes, u_inverse, preferred_element_type=jnp.float32)
    def power(step, carry):
        current, series_sum = carry
        panel = a2a_gather(current.astype(jnp.bfloat16), "lmk")
        tile_rows = jnp.take(panel, tile_cam, axis=0)
        forward = jnp.einsum(
            "tpc,tcl->tpl", tile_rows, couplings, preferred_element_type=jnp.float32
        )
        partial_value = onehot_sum(lmk_onehot, forward)
        landmark_part = cam_reduce(partial_value)
        landmark_part_out = jnp.einsum(
            "mpl,mlq->mpq",
            landmark_part.astype(jnp.bfloat16),
            v_part,
            preferred_element_type=jnp.float32,
        ).astype(jnp.bfloat16)
        landmark_out = cam_gather(landmark_part_out)
        picked = jnp.take(landmark_out, tile_lmk, axis=0)
        backward = jnp.einsum("tpl,tcl->tpc", picked, couplings, preferred_element_type=jnp.float32)
        camera_sum = a2a_reduce_scatter(onehot_sum(cam_onehot, backward), "lmk")
        current = jnp.einsum(
            "bpc,bcd->bpd",
            camera_sum.astype(jnp.bfloat16),
            u_inverse,
            preferred_element_type=jnp.float32,
        )
        return current, series_sum + current

    _, series_sum = lax.fori_loop(0, POWERS, power, (current, current))
    return series_sum


def solution(mesh):
    COLLECTIVE_IDS.clear()
    in_specs = (
        P(("cam", "lmk"), None, None),
        P(("cam", "lmk"), None, None),
        P(("cam", "lmk"), None, None),
        P("lmk", None, None),
        P(("cam", "lmk")),
        P(("cam", "lmk")),
    )
    out_specs = P(("cam", "lmk"), None, None)
    return jax.shard_map(local, mesh=mesh, in_specs=in_specs, out_specs=out_specs, check_vma=False)
```

```python
import functools

import jax
import jax.numpy as jnp
from jax import lax
from jax.experimental import pallas as pl
from jax.experimental.pallas import tpu as pltpu
from jax.sharding import PartitionSpec as P

POWERS = 4
MESH = pl.DeviceIdType.MESH
AXES = ("cam", "lmk")
COLLECTIVE_IDS = {}


def exchange_kernel(n, axis, gather, x_ref, o_ref, send_sem, recv_sem, local_sem):
    me = lax.axis_index(axis)
    coords = tuple(lax.axis_index(name) for name in AXES)
    slot = AXES.index(axis)

    def device(peer):
        return coords[:slot] + (peer,) + coords[slot + 1:]

    barrier = pltpu.get_barrier_semaphore()
    for step in range(1, n):
        pl.semaphore_signal(barrier, inc=1, device_id=device(lax.rem(me + step, n)), device_id_type=MESH)
    pl.semaphore_wait(barrier, n - 1)
    local = pltpu.make_async_copy(x_ref if gather else x_ref.at[me], o_ref.at[me], local_sem)
    local.start()
    sends = []
    for step in range(1, n):
        peer = lax.rem(me + step, n)
        copy = pltpu.make_async_remote_copy(
            src_ref=x_ref if gather else x_ref.at[peer],
            dst_ref=o_ref.at[me],
            send_sem=send_sem.at[step],
            recv_sem=recv_sem.at[step],
            device_id=device(peer),
            device_id_type=MESH,
        )
        copy.start()
        sends.append(copy)
    local.wait()
    for copy in sends:
        copy.wait_send()
    for step in range(1, n):
        source = lax.rem(me + n - step, n)
        pltpu.make_async_remote_copy(
            src_ref=o_ref.at[source],
            dst_ref=o_ref.at[source],
            send_sem=send_sem.at[step],
            recv_sem=recv_sem.at[step],
            device_id=device(source),
            device_id_type=MESH,
        ).wait_recv()


def exchange(x, axis_name, gather=False):
    n = lax.axis_size(axis_name)
    key = (axis_name, gather, x.shape, str(x.dtype))
    if key not in COLLECTIVE_IDS:
        COLLECTIVE_IDS[key] = len(COLLECTIVE_IDS)
    shape = (n,) + x.shape if gather else x.shape
    return pl.pallas_call(
        functools.partial(exchange_kernel, n, axis_name, gather),
        out_shape=jax.ShapeDtypeStruct(shape, x.dtype),
        in_specs=[pl.BlockSpec(memory_space=pl.ANY)],
        out_specs=pl.BlockSpec(memory_space=pl.ANY),
        scratch_shapes=[
            pltpu.SemaphoreType.DMA((n,)),
            pltpu.SemaphoreType.DMA((n,)),
            pltpu.SemaphoreType.DMA,
        ],
        compiler_params=pltpu.CompilerParams(collective_id=COLLECTIVE_IDS[key], has_side_effects=True),
    )(x)


def onehot_sum(selected, values):
    upper = values.astype(jnp.bfloat16)
    lower = (values - upper.astype(jnp.float32)).astype(jnp.bfloat16)
    first = jnp.einsum("st,tpx->spx", selected, upper, preferred_element_type=jnp.float32)
    second = jnp.einsum("st,tpx->spx", selected, lower, preferred_element_type=jnp.float32)
    return first + second


def a2a_gather(block, axis_name):
    size = lax.axis_size(axis_name)
    if axis_name == "cam":
        got = exchange(block, axis_name, gather=True)
    else:
        tiled = jnp.broadcast_to(block[None], (size,) + block.shape)
        got = lax.all_to_all(tiled, axis_name, 0, 0, tiled=False)
    return got.reshape((size * block.shape[0],) + block.shape[1:])


def a2a_reduce_scatter(full, axis_name):
    size = lax.axis_size(axis_name)
    chunks = full.reshape((size, full.shape[0] // size) + full.shape[1:])
    if axis_name == "cam":
        got = exchange(chunks.astype(jnp.bfloat16), axis_name)
    else:
        got = lax.all_to_all(chunks.astype(jnp.bfloat16), axis_name, 0, 0, tiled=False)
    return jnp.sum(got.astype(jnp.float32), axis=0)


def swap_kernel(x_ref, o_ref, send_sem, recv_sem, *, partner):
    barrier = pltpu.get_barrier_semaphore()
    pl.semaphore_signal(barrier, inc=1, device_id=partner(), device_id_type=MESH)
    pl.semaphore_wait(barrier, 1)
    copy = pltpu.make_async_remote_copy(
        src_ref=x_ref,
        dst_ref=o_ref,
        send_sem=send_sem,
        recv_sem=recv_sem,
        device_id=partner(),
        device_id_type=MESH,
    )
    copy.start()
    copy.wait_send()
    copy.wait_recv()


def swap(x, flip):
    key = ("swap", flip, x.shape, str(x.dtype))
    if key not in COLLECTIVE_IDS:
        COLLECTIVE_IDS[key] = len(COLLECTIVE_IDS)

    def partner():
        return (lax.axis_index("cam") ^ flip, lax.axis_index("lmk"))

    return pl.pallas_call(
        functools.partial(swap_kernel, partner=partner),
        out_shape=jax.ShapeDtypeStruct(x.shape, x.dtype),
        in_specs=[pl.BlockSpec(memory_space=pl.ANY)],
        out_specs=pl.BlockSpec(memory_space=pl.ANY),
        scratch_shapes=[pltpu.SemaphoreType.DMA, pltpu.SemaphoreType.DMA],
        compiler_params=pltpu.CompilerParams(collective_id=COLLECTIVE_IDS[key], has_side_effects=True),
    )(x)


def pick(flag, a, b):
    return jnp.where(flag == 0, a, b)


def cam_reduce(partial_value):
    cam = lax.axis_index("cam")
    core, high = cam % 2, cam // 2
    chunks = partial_value.reshape((2, 2, partial_value.shape[0] // 4) + partial_value.shape[1:])
    mine = pick(core, chunks[:, 0], chunks[:, 1])
    theirs = pick(core, chunks[:, 1], chunks[:, 0])
    chip = mine + swap(theirs.astype(jnp.bfloat16), 1).astype(jnp.float32)
    keep = pick(high, chip[0], chip[1])
    send = pick(high, chip[1], chip[0])
    return keep + swap(send.astype(jnp.bfloat16), 2).astype(jnp.float32)


def cam_gather_kernel(x_ref, o_ref, send_sem, recv_sem, local_sem):
    cam = lax.axis_index("cam")
    lmk = lax.axis_index("lmk")
    core_peer, high_peer = cam ^ 1, cam ^ 2
    barrier = pltpu.get_barrier_semaphore()
    for peer in (core_peer, high_peer):
        pl.semaphore_signal(barrier, inc=1, device_id=(peer, lmk), device_id_type=MESH)
    pl.semaphore_wait(barrier, 2)

    def remote(src, dst, slot, peer):
        return pltpu.make_async_remote_copy(
            src_ref=src,
            dst_ref=dst,
            send_sem=send_sem.at[slot],
            recv_sem=recv_sem.at[slot],
            device_id=(peer, lmk),
            device_id_type=MESH,
        )

    local = pltpu.make_async_copy(x_ref, o_ref.at[cam], local_sem)
    local.start()
    to_high = remote(x_ref, o_ref.at[cam], 0, high_peer)
    to_high.start()
    to_core = remote(x_ref, o_ref.at[cam], 1, core_peer)
    to_core.start()
    remote(o_ref.at[high_peer], o_ref.at[high_peer], 0, high_peer).wait_recv()
    relay = remote(o_ref.at[high_peer], o_ref.at[high_peer], 2, core_peer)
    relay.start()
    local.wait()
    to_high.wait_send()
    to_core.wait_send()
    relay.wait_send()
    remote(o_ref.at[core_peer], o_ref.at[core_peer], 1, core_peer).wait_recv()
    remote(o_ref.at[cam ^ 3], o_ref.at[cam ^ 3], 2, core_peer).wait_recv()


def cam_gather(block):
    key = ("cam_gather", block.shape, str(block.dtype))
    if key not in COLLECTIVE_IDS:
        COLLECTIVE_IDS[key] = len(COLLECTIVE_IDS)
    full = pl.pallas_call(
        cam_gather_kernel,
        out_shape=jax.ShapeDtypeStruct((4,) + block.shape, block.dtype),
        in_specs=[pl.BlockSpec(memory_space=pl.ANY)],
        out_specs=pl.BlockSpec(memory_space=pl.ANY),
        scratch_shapes=[
            pltpu.SemaphoreType.DMA((3,)),
            pltpu.SemaphoreType.DMA((3,)),
            pltpu.SemaphoreType.DMA,
        ],
        compiler_params=pltpu.CompilerParams(collective_id=COLLECTIVE_IDS[key], has_side_effects=True),
    )(block)
    return full.reshape((4 * block.shape[0],) + block.shape[1:])


def local(probes, u_inverse, couplings, v_inverse, tile_cam, tile_lmk):
    group_size = lax.axis_size("lmk") * u_inverse.shape[0]
    landmark_count = v_inverse.shape[0]
    cam_onehot = (tile_cam[None, :] == jnp.arange(group_size, dtype=jnp.int32)[:, None]).astype(
        jnp.bfloat16
    )
    lmk_onehot = (tile_lmk[None, :] == jnp.arange(landmark_count, dtype=jnp.int32)[:, None]).astype(
        jnp.bfloat16
    )
    cam_count = lax.axis_size("cam")
    part_size = landmark_count // cam_count
    v_part = lax.dynamic_slice_in_dim(v_inverse, lax.axis_index("cam") * part_size, part_size, 0)
    current = jnp.einsum("bpc,bcd->bpd", probes, u_inverse, preferred_element_type=jnp.float32)
    series_sum = current
    panel = a2a_gather(current.astype(jnp.bfloat16), "lmk")
    for power_step in range(POWERS):
        tile_rows = jnp.take(panel, tile_cam, axis=0)
        forward = jnp.einsum(
            "tpc,tcl->tpl", tile_rows, couplings, preferred_element_type=jnp.float32
        )
        partial_value = onehot_sum(lmk_onehot, forward)
        landmark_part = cam_reduce(partial_value)
        landmark_part_out = jnp.einsum(
            "mpl,mlq->mpq",
            landmark_part.astype(jnp.bfloat16),
            v_part,
            preferred_element_type=jnp.float32,
        ).astype(jnp.bfloat16)
        landmark_out = cam_gather(landmark_part_out)
        picked = jnp.take(landmark_out, tile_lmk, axis=0)
        backward = jnp.einsum("tpl,tcl->tpc", picked, couplings, preferred_element_type=jnp.float32)
        camera_sum = a2a_reduce_scatter(onehot_sum(cam_onehot, backward), "lmk")
        current = jnp.einsum(
            "bpc,bcd->bpd",
            camera_sum.astype(jnp.bfloat16),
            u_inverse,
            preferred_element_type=jnp.float32,
        )
        series_sum = series_sum + current
        if power_step + 1 < POWERS:
            panel = a2a_gather(current.astype(jnp.bfloat16), "lmk")
    return series_sum


def solution(mesh):
    COLLECTIVE_IDS.clear()
    in_specs = (
        P(("cam", "lmk"), None, None),
        P(("cam", "lmk"), None, None),
        P(("cam", "lmk"), None, None),
        P("lmk", None, None),
        P(("cam", "lmk")),
        P(("cam", "lmk")),
    )
    out_specs = P(("cam", "lmk"), None, None)
    return jax.shard_map(local, mesh=mesh, in_specs=in_specs, out_specs=out_specs, check_vma=False)
```

```python
import functools

import jax
import jax.numpy as jnp
from jax import lax
from jax.experimental import pallas as pl
from jax.experimental.pallas import tpu as pltpu
from jax.sharding import PartitionSpec as P

POWERS = 4
MESH = pl.DeviceIdType.MESH
AXES = ("cam", "lmk")
COLLECTIVE_IDS = {}


def exchange_kernel(n, axis, gather, x_ref, o_ref, send_sem, recv_sem, local_sem):
    me = lax.axis_index(axis)
    coords = tuple(lax.axis_index(name) for name in AXES)
    slot = AXES.index(axis)

    def device(peer):
        return coords[:slot] + (peer,) + coords[slot + 1:]

    barrier = pltpu.get_barrier_semaphore()
    for step in range(1, n):
        pl.semaphore_signal(barrier, inc=1, device_id=device(lax.rem(me + step, n)), device_id_type=MESH)
    pl.semaphore_wait(barrier, n - 1)
    local = pltpu.make_async_copy(x_ref if gather else x_ref.at[me], o_ref.at[me], local_sem)
    local.start()
    sends = []
    for step in range(1, n):
        peer = lax.rem(me + step, n)
        copy = pltpu.make_async_remote_copy(
            src_ref=x_ref if gather else x_ref.at[peer],
            dst_ref=o_ref.at[me],
            send_sem=send_sem.at[step],
            recv_sem=recv_sem.at[step],
            device_id=device(peer),
            device_id_type=MESH,
        )
        copy.start()
        sends.append(copy)
    local.wait()
    for copy in sends:
        copy.wait_send()
    for step in range(1, n):
        source = lax.rem(me + n - step, n)
        pltpu.make_async_remote_copy(
            src_ref=o_ref.at[source],
            dst_ref=o_ref.at[source],
            send_sem=send_sem.at[step],
            recv_sem=recv_sem.at[step],
            device_id=device(source),
            device_id_type=MESH,
        ).wait_recv()


def exchange(x, axis_name, gather=False):
    n = lax.axis_size(axis_name)
    key = (axis_name, gather, x.shape, str(x.dtype))
    if key not in COLLECTIVE_IDS:
        COLLECTIVE_IDS[key] = len(COLLECTIVE_IDS)
    shape = (n,) + x.shape if gather else x.shape
    return pl.pallas_call(
        functools.partial(exchange_kernel, n, axis_name, gather),
        out_shape=jax.ShapeDtypeStruct(shape, x.dtype),
        in_specs=[pl.BlockSpec(memory_space=pl.ANY)],
        out_specs=pl.BlockSpec(memory_space=pl.ANY),
        scratch_shapes=[
            pltpu.SemaphoreType.DMA((n,)),
            pltpu.SemaphoreType.DMA((n,)),
            pltpu.SemaphoreType.DMA,
        ],
        compiler_params=pltpu.CompilerParams(collective_id=COLLECTIVE_IDS[key], has_side_effects=True),
    )(x)


def onehot_sum(selected, values):
    upper = values.astype(jnp.bfloat16)
    lower = (values - upper.astype(jnp.float32)).astype(jnp.bfloat16)
    first = jnp.einsum("st,tpx->spx", selected, upper, preferred_element_type=jnp.float32)
    second = jnp.einsum("st,tpx->spx", selected, lower, preferred_element_type=jnp.float32)
    return first + second


def a2a_gather(block, axis_name):
    size = lax.axis_size(axis_name)
    if axis_name == "cam":
        got = exchange(block, axis_name, gather=True)
    else:
        tiled = jnp.broadcast_to(block[None], (size,) + block.shape)
        got = lax.all_to_all(tiled, axis_name, 0, 0, tiled=False)
    return got.reshape((size * block.shape[0],) + block.shape[1:])


def a2a_reduce_scatter(full, axis_name):
    size = lax.axis_size(axis_name)
    chunks = full.reshape((size, full.shape[0] // size) + full.shape[1:])
    if axis_name == "cam":
        got = exchange(chunks.astype(jnp.bfloat16), axis_name)
    else:
        got = lax.all_to_all(chunks.astype(jnp.bfloat16), axis_name, 0, 0, tiled=False)
    return jnp.sum(got.astype(jnp.float32), axis=0)


def swap_kernel(x_ref, o_ref, send_sem, recv_sem, *, partner):
    barrier = pltpu.get_barrier_semaphore()
    pl.semaphore_signal(barrier, inc=1, device_id=partner(), device_id_type=MESH)
    pl.semaphore_wait(barrier, 1)
    copy = pltpu.make_async_remote_copy(
        src_ref=x_ref,
        dst_ref=o_ref,
        send_sem=send_sem,
        recv_sem=recv_sem,
        device_id=partner(),
        device_id_type=MESH,
    )
    copy.start()
    copy.wait_send()
    copy.wait_recv()


def swap(x, flip):
    key = ("swap", flip, x.shape, str(x.dtype))
    if key not in COLLECTIVE_IDS:
        COLLECTIVE_IDS[key] = len(COLLECTIVE_IDS)

    def partner():
        return (lax.axis_index("cam") ^ flip, lax.axis_index("lmk"))

    return pl.pallas_call(
        functools.partial(swap_kernel, partner=partner),
        out_shape=jax.ShapeDtypeStruct(x.shape, x.dtype),
        in_specs=[pl.BlockSpec(memory_space=pl.ANY)],
        out_specs=pl.BlockSpec(memory_space=pl.ANY),
        scratch_shapes=[pltpu.SemaphoreType.DMA, pltpu.SemaphoreType.DMA],
        compiler_params=pltpu.CompilerParams(collective_id=COLLECTIVE_IDS[key], has_side_effects=True),
    )(x)


def pick(flag, a, b):
    return jnp.where(flag == 0, a, b)


def cam_reduce_kernel(x_ref, o_ref, send_one, recv_one, chip_ref, send_two, recv_two, send_sem, recv_sem):
    cam = lax.axis_index("cam")
    lmk = lax.axis_index("lmk")
    core, high = cam % 2, cam // 2
    core_peer, high_peer = cam ^ 1, cam ^ 2
    send_one[...] = x_ref[1 - core].astype(send_one.dtype)
    barrier = pltpu.get_barrier_semaphore()
    for peer in (core_peer, high_peer):
        pl.semaphore_signal(barrier, inc=1, device_id=(peer, lmk), device_id_type=MESH)
    pl.semaphore_wait(barrier, 2)
    first = pltpu.make_async_remote_copy(
        src_ref=send_one,
        dst_ref=recv_one,
        send_sem=send_sem.at[0],
        recv_sem=recv_sem.at[0],
        device_id=(core_peer, lmk),
        device_id_type=MESH,
    )
    first.start()
    first.wait_send()
    first.wait_recv()
    chip_ref[...] = x_ref[core] + recv_one[...].astype(jnp.float32)
    send_two[...] = chip_ref[1 - high].astype(send_two.dtype)
    second = pltpu.make_async_remote_copy(
        src_ref=send_two,
        dst_ref=recv_two,
        send_sem=send_sem.at[1],
        recv_sem=recv_sem.at[1],
        device_id=(high_peer, lmk),
        device_id_type=MESH,
    )
    second.start()
    second.wait_send()
    second.wait_recv()
    o_ref[...] = chip_ref[high] + recv_two[...].astype(jnp.float32)


def cam_reduce(partial_value):
    chunk = partial_value.shape[0] // 4
    rest = partial_value.shape[1:]
    chunks = partial_value.reshape((2, 2, chunk) + rest).swapaxes(0, 1)
    key = ("cam_reduce", chunks.shape)
    if key not in COLLECTIVE_IDS:
        COLLECTIVE_IDS[key] = len(COLLECTIVE_IDS)
    return pl.pallas_call(
        cam_reduce_kernel,
        out_shape=jax.ShapeDtypeStruct((chunk,) + rest, jnp.float32),
        in_specs=[pl.BlockSpec(memory_space=pltpu.VMEM)],
        out_specs=pl.BlockSpec(memory_space=pltpu.VMEM),
        scratch_shapes=[
            pltpu.VMEM((2, chunk) + rest, jnp.bfloat16),
            pltpu.VMEM((2, chunk) + rest, jnp.bfloat16),
            pltpu.VMEM((2, chunk) + rest, jnp.float32),
            pltpu.VMEM((chunk,) + rest, jnp.bfloat16),
            pltpu.VMEM((chunk,) + rest, jnp.bfloat16),
            pltpu.SemaphoreType.DMA((2,)),
            pltpu.SemaphoreType.DMA((2,)),
        ],
        compiler_params=pltpu.CompilerParams(collective_id=COLLECTIVE_IDS[key], has_side_effects=True),
    )(chunks)


def cam_gather_kernel(x_ref, o_ref, send_sem, recv_sem, local_sem):
    cam = lax.axis_index("cam")
    lmk = lax.axis_index("lmk")
    core_peer, high_peer = cam ^ 1, cam ^ 2
    barrier = pltpu.get_barrier_semaphore()
    for peer in (core_peer, high_peer):
        pl.semaphore_signal(barrier, inc=1, device_id=(peer, lmk), device_id_type=MESH)
    pl.semaphore_wait(barrier, 2)

    def remote(src, dst, slot, peer):
        return pltpu.make_async_remote_copy(
            src_ref=src,
            dst_ref=dst,
            send_sem=send_sem.at[slot],
            recv_sem=recv_sem.at[slot],
            device_id=(peer, lmk),
            device_id_type=MESH,
        )

    local = pltpu.make_async_copy(x_ref, o_ref.at[cam], local_sem)
    local.start()
    to_high = remote(x_ref, o_ref.at[cam], 0, high_peer)
    to_high.start()
    to_core = remote(x_ref, o_ref.at[cam], 1, core_peer)
    to_core.start()
    remote(o_ref.at[high_peer], o_ref.at[high_peer], 0, high_peer).wait_recv()
    relay = remote(o_ref.at[high_peer], o_ref.at[high_peer], 2, core_peer)
    relay.start()
    local.wait()
    to_high.wait_send()
    to_core.wait_send()
    relay.wait_send()
    remote(o_ref.at[core_peer], o_ref.at[core_peer], 1, core_peer).wait_recv()
    remote(o_ref.at[cam ^ 3], o_ref.at[cam ^ 3], 2, core_peer).wait_recv()


def cam_gather(block):
    key = ("cam_gather", block.shape, str(block.dtype))
    if key not in COLLECTIVE_IDS:
        COLLECTIVE_IDS[key] = len(COLLECTIVE_IDS)
    full = pl.pallas_call(
        cam_gather_kernel,
        out_shape=jax.ShapeDtypeStruct((4,) + block.shape, block.dtype),
        in_specs=[pl.BlockSpec(memory_space=pl.ANY)],
        out_specs=pl.BlockSpec(memory_space=pl.ANY),
        scratch_shapes=[
            pltpu.SemaphoreType.DMA((3,)),
            pltpu.SemaphoreType.DMA((3,)),
            pltpu.SemaphoreType.DMA,
        ],
        compiler_params=pltpu.CompilerParams(collective_id=COLLECTIVE_IDS[key], has_side_effects=True),
    )(block)
    return full.reshape((4 * block.shape[0],) + block.shape[1:])


def local(probes, u_inverse, couplings, v_inverse, tile_cam, tile_lmk):
    group_size = lax.axis_size("lmk") * u_inverse.shape[0]
    landmark_count = v_inverse.shape[0]
    cam_onehot = (tile_cam[None, :] == jnp.arange(group_size, dtype=jnp.int32)[:, None]).astype(
        jnp.bfloat16
    )
    lmk_onehot = (tile_lmk[None, :] == jnp.arange(landmark_count, dtype=jnp.int32)[:, None]).astype(
        jnp.bfloat16
    )
    cam_count = lax.axis_size("cam")
    part_size = landmark_count // cam_count
    v_part = lax.dynamic_slice_in_dim(v_inverse, lax.axis_index("cam") * part_size, part_size, 0)
    current = jnp.einsum("bpc,bcd->bpd", probes, u_inverse, preferred_element_type=jnp.float32)
    series_sum = current
    panel = a2a_gather(current.astype(jnp.bfloat16), "lmk")
    for power_step in range(POWERS):
        tile_rows = jnp.take(panel, tile_cam, axis=0)
        forward = jnp.einsum(
            "tpc,tcl->tpl", tile_rows, couplings, preferred_element_type=jnp.float32
        )
        partial_value = onehot_sum(lmk_onehot, forward)
        landmark_part = cam_reduce(partial_value)
        landmark_part_out = jnp.einsum(
            "mpl,mlq->mpq",
            landmark_part.astype(jnp.bfloat16),
            v_part,
            preferred_element_type=jnp.float32,
        ).astype(jnp.bfloat16)
        landmark_out = cam_gather(landmark_part_out)
        picked = jnp.take(landmark_out, tile_lmk, axis=0)
        backward = jnp.einsum("tpl,tcl->tpc", picked, couplings, preferred_element_type=jnp.float32)
        camera_sum = a2a_reduce_scatter(onehot_sum(cam_onehot, backward), "lmk")
        current = jnp.einsum(
            "bpc,bcd->bpd",
            camera_sum.astype(jnp.bfloat16),
            u_inverse,
            preferred_element_type=jnp.float32,
        )
        series_sum = series_sum + current
        if power_step + 1 < POWERS:
            panel = a2a_gather(current.astype(jnp.bfloat16), "lmk")
    return series_sum


def solution(mesh):
    COLLECTIVE_IDS.clear()
    in_specs = (
        P(("cam", "lmk"), None, None),
        P(("cam", "lmk"), None, None),
        P(("cam", "lmk"), None, None),
        P("lmk", None, None),
        P(("cam", "lmk")),
        P(("cam", "lmk")),
    )
    out_specs = P(("cam", "lmk"), None, None)
    return jax.shard_map(local, mesh=mesh, in_specs=in_specs, out_specs=out_specs, check_vma=False)
```

```python
import functools

import jax
import jax.numpy as jnp
from jax import lax
from jax.experimental import pallas as pl
from jax.experimental.pallas import tpu as pltpu
from jax.sharding import PartitionSpec as P

POWERS = 4
MESH = pl.DeviceIdType.MESH
AXES = ("cam", "lmk")
COLLECTIVE_IDS = {}


def exchange_kernel(n, axis, gather, x_ref, o_ref, send_sem, recv_sem, local_sem):
    me = lax.axis_index(axis)
    coords = tuple(lax.axis_index(name) for name in AXES)
    slot = AXES.index(axis)

    def device(peer):
        return coords[:slot] + (peer,) + coords[slot + 1:]

    barrier = pltpu.get_barrier_semaphore()
    for step in range(1, n):
        pl.semaphore_signal(barrier, inc=1, device_id=device(lax.rem(me + step, n)), device_id_type=MESH)
    pl.semaphore_wait(barrier, n - 1)
    local = pltpu.make_async_copy(x_ref if gather else x_ref.at[me], o_ref.at[me], local_sem)
    local.start()
    sends = []
    for step in range(1, n):
        peer = lax.rem(me + step, n)
        copy = pltpu.make_async_remote_copy(
            src_ref=x_ref if gather else x_ref.at[peer],
            dst_ref=o_ref.at[me],
            send_sem=send_sem.at[step],
            recv_sem=recv_sem.at[step],
            device_id=device(peer),
            device_id_type=MESH,
        )
        copy.start()
        sends.append(copy)
    local.wait()
    for copy in sends:
        copy.wait_send()
    for step in range(1, n):
        source = lax.rem(me + n - step, n)
        pltpu.make_async_remote_copy(
            src_ref=o_ref.at[source],
            dst_ref=o_ref.at[source],
            send_sem=send_sem.at[step],
            recv_sem=recv_sem.at[step],
            device_id=device(source),
            device_id_type=MESH,
        ).wait_recv()


def exchange(x, axis_name, gather=False):
    n = lax.axis_size(axis_name)
    key = (axis_name, gather, x.shape, str(x.dtype))
    if key not in COLLECTIVE_IDS:
        COLLECTIVE_IDS[key] = len(COLLECTIVE_IDS)
    shape = (n,) + x.shape if gather else x.shape
    return pl.pallas_call(
        functools.partial(exchange_kernel, n, axis_name, gather),
        out_shape=jax.ShapeDtypeStruct(shape, x.dtype),
        in_specs=[pl.BlockSpec(memory_space=pl.ANY)],
        out_specs=pl.BlockSpec(memory_space=pl.ANY),
        scratch_shapes=[
            pltpu.SemaphoreType.DMA((n,)),
            pltpu.SemaphoreType.DMA((n,)),
            pltpu.SemaphoreType.DMA,
        ],
        compiler_params=pltpu.CompilerParams(collective_id=COLLECTIVE_IDS[key], has_side_effects=True),
    )(x)


def onehot_sum(selected, values):
    return jnp.einsum(
        "st,tpx->spx", selected, values.astype(jnp.bfloat16), preferred_element_type=jnp.float32
    )


def a2a_gather(block, axis_name):
    size = lax.axis_size(axis_name)
    if axis_name == "cam":
        got = exchange(block, axis_name, gather=True)
    else:
        tiled = jnp.broadcast_to(block[None], (size,) + block.shape)
        got = lax.all_to_all(tiled, axis_name, 0, 0, tiled=False)
    return got.reshape((size * block.shape[0],) + block.shape[1:])


def a2a_reduce_scatter(full, axis_name):
    size = lax.axis_size(axis_name)
    chunks = full.reshape((size, full.shape[0] // size) + full.shape[1:])
    if axis_name == "cam":
        got = exchange(chunks.astype(jnp.bfloat16), axis_name)
    else:
        got = lax.all_to_all(chunks.astype(jnp.bfloat16), axis_name, 0, 0, tiled=False)
    return jnp.sum(got.astype(jnp.float32), axis=0)


def swap_kernel(x_ref, o_ref, send_sem, recv_sem, *, partner):
    barrier = pltpu.get_barrier_semaphore()
    pl.semaphore_signal(barrier, inc=1, device_id=partner(), device_id_type=MESH)
    pl.semaphore_wait(barrier, 1)
    copy = pltpu.make_async_remote_copy(
        src_ref=x_ref,
        dst_ref=o_ref,
        send_sem=send_sem,
        recv_sem=recv_sem,
        device_id=partner(),
        device_id_type=MESH,
    )
    copy.start()
    copy.wait_send()
    copy.wait_recv()


def swap(x, flip):
    key = ("swap", flip, x.shape, str(x.dtype))
    if key not in COLLECTIVE_IDS:
        COLLECTIVE_IDS[key] = len(COLLECTIVE_IDS)

    def partner():
        return (lax.axis_index("cam") ^ flip, lax.axis_index("lmk"))

    return pl.pallas_call(
        functools.partial(swap_kernel, partner=partner),
        out_shape=jax.ShapeDtypeStruct(x.shape, x.dtype),
        in_specs=[pl.BlockSpec(memory_space=pl.ANY)],
        out_specs=pl.BlockSpec(memory_space=pl.ANY),
        scratch_shapes=[pltpu.SemaphoreType.DMA, pltpu.SemaphoreType.DMA],
        compiler_params=pltpu.CompilerParams(collective_id=COLLECTIVE_IDS[key], has_side_effects=True),
    )(x)


def pick(flag, a, b):
    return jnp.where(flag == 0, a, b)


def cam_reduce(partial_value):
    cam = lax.axis_index("cam")
    core, high = cam % 2, cam // 2
    chunks = partial_value.reshape((2, 2, partial_value.shape[0] // 4) + partial_value.shape[1:])
    mine = pick(core, chunks[:, 0], chunks[:, 1])
    theirs = pick(core, chunks[:, 1], chunks[:, 0])
    chip = mine + swap(theirs.astype(jnp.bfloat16), 1).astype(jnp.float32)
    keep = pick(high, chip[0], chip[1])
    send = pick(high, chip[1], chip[0])
    return keep + swap(send.astype(jnp.bfloat16), 2).astype(jnp.float32)


def cam_gather_kernel(x_ref, o_ref, send_sem, recv_sem, local_sem):
    cam = lax.axis_index("cam")
    lmk = lax.axis_index("lmk")
    core_peer, high_peer = cam ^ 1, cam ^ 2
    barrier = pltpu.get_barrier_semaphore()
    for peer in (core_peer, high_peer):
        pl.semaphore_signal(barrier, inc=1, device_id=(peer, lmk), device_id_type=MESH)
    pl.semaphore_wait(barrier, 2)

    def remote(src, dst, slot, peer):
        return pltpu.make_async_remote_copy(
            src_ref=src,
            dst_ref=dst,
            send_sem=send_sem.at[slot],
            recv_sem=recv_sem.at[slot],
            device_id=(peer, lmk),
            device_id_type=MESH,
        )

    local = pltpu.make_async_copy(x_ref, o_ref.at[cam], local_sem)
    local.start()
    to_high = remote(x_ref, o_ref.at[cam], 0, high_peer)
    to_high.start()
    to_core = remote(x_ref, o_ref.at[cam], 1, core_peer)
    to_core.start()
    remote(o_ref.at[high_peer], o_ref.at[high_peer], 0, high_peer).wait_recv()
    relay = remote(o_ref.at[high_peer], o_ref.at[high_peer], 2, core_peer)
    relay.start()
    local.wait()
    to_high.wait_send()
    to_core.wait_send()
    relay.wait_send()
    remote(o_ref.at[core_peer], o_ref.at[core_peer], 1, core_peer).wait_recv()
    remote(o_ref.at[cam ^ 3], o_ref.at[cam ^ 3], 2, core_peer).wait_recv()


def cam_gather(block):
    key = ("cam_gather", block.shape, str(block.dtype))
    if key not in COLLECTIVE_IDS:
        COLLECTIVE_IDS[key] = len(COLLECTIVE_IDS)
    full = pl.pallas_call(
        cam_gather_kernel,
        out_shape=jax.ShapeDtypeStruct((4,) + block.shape, block.dtype),
        in_specs=[pl.BlockSpec(memory_space=pl.ANY)],
        out_specs=pl.BlockSpec(memory_space=pl.ANY),
        scratch_shapes=[
            pltpu.SemaphoreType.DMA((3,)),
            pltpu.SemaphoreType.DMA((3,)),
            pltpu.SemaphoreType.DMA,
        ],
        compiler_params=pltpu.CompilerParams(collective_id=COLLECTIVE_IDS[key], has_side_effects=True),
    )(block)
    return full.reshape((4 * block.shape[0],) + block.shape[1:])


def local(probes, u_inverse, couplings, v_inverse, tile_cam, tile_lmk):
    group_size = lax.axis_size("lmk") * u_inverse.shape[0]
    landmark_count = v_inverse.shape[0]
    cam_onehot = (tile_cam[None, :] == jnp.arange(group_size, dtype=jnp.int32)[:, None]).astype(
        jnp.bfloat16
    )
    lmk_onehot = (tile_lmk[None, :] == jnp.arange(landmark_count, dtype=jnp.int32)[:, None]).astype(
        jnp.bfloat16
    )
    cam_count = lax.axis_size("cam")
    part_size = landmark_count // cam_count
    v_part = lax.dynamic_slice_in_dim(v_inverse, lax.axis_index("cam") * part_size, part_size, 0)
    current = jnp.einsum("bpc,bcd->bpd", probes, u_inverse, preferred_element_type=jnp.float32)
    series_sum = current
    panel = a2a_gather(current.astype(jnp.bfloat16), "lmk")
    for power_step in range(POWERS):
        tile_rows = jnp.take(panel, tile_cam, axis=0)
        forward = jnp.einsum(
            "tpc,tcl->tpl", tile_rows, couplings, preferred_element_type=jnp.float32
        )
        partial_value = onehot_sum(lmk_onehot, forward)
        landmark_part = cam_reduce(partial_value)
        landmark_part_out = jnp.einsum(
            "mpl,mlq->mpq",
            landmark_part.astype(jnp.bfloat16),
            v_part,
            preferred_element_type=jnp.float32,
        ).astype(jnp.bfloat16)
        landmark_out = cam_gather(landmark_part_out)
        picked = jnp.take(landmark_out, tile_lmk, axis=0)
        backward = jnp.einsum("tpl,tcl->tpc", picked, couplings, preferred_element_type=jnp.float32)
        camera_sum = a2a_reduce_scatter(onehot_sum(cam_onehot, backward), "lmk")
        current = jnp.einsum(
            "bpc,bcd->bpd",
            camera_sum.astype(jnp.bfloat16),
            u_inverse,
            preferred_element_type=jnp.float32,
        )
        series_sum = series_sum + current
        if power_step + 1 < POWERS:
            panel = a2a_gather(current.astype(jnp.bfloat16), "lmk")
    return series_sum


def solution(mesh):
    COLLECTIVE_IDS.clear()
    in_specs = (
        P(("cam", "lmk"), None, None),
        P(("cam", "lmk"), None, None),
        P(("cam", "lmk"), None, None),
        P("lmk", None, None),
        P(("cam", "lmk")),
        P(("cam", "lmk")),
    )
    out_specs = P(("cam", "lmk"), None, None)
    return jax.shard_map(local, mesh=mesh, in_specs=in_specs, out_specs=out_specs, check_vma=False)
```

```python
import functools

import jax
import jax.numpy as jnp
from jax import lax
from jax.experimental import pallas as pl
from jax.experimental.pallas import tpu as pltpu
from jax.sharding import PartitionSpec as P

POWERS = 4
MESH = pl.DeviceIdType.MESH
AXES = ("cam", "lmk")
COLLECTIVE_IDS = {}


def exchange_kernel(n, axis, gather, x_ref, o_ref, send_sem, recv_sem, local_sem):
    me = lax.axis_index(axis)
    coords = tuple(lax.axis_index(name) for name in AXES)
    slot = AXES.index(axis)

    def device(peer):
        return coords[:slot] + (peer,) + coords[slot + 1:]

    barrier = pltpu.get_barrier_semaphore()
    for step in range(1, n):
        pl.semaphore_signal(barrier, inc=1, device_id=device(lax.rem(me + step, n)), device_id_type=MESH)
    pl.semaphore_wait(barrier, n - 1)
    local = pltpu.make_async_copy(x_ref if gather else x_ref.at[me], o_ref.at[me], local_sem)
    local.start()
    sends = []
    for step in range(1, n):
        peer = lax.rem(me + step, n)
        copy = pltpu.make_async_remote_copy(
            src_ref=x_ref if gather else x_ref.at[peer],
            dst_ref=o_ref.at[me],
            send_sem=send_sem.at[step],
            recv_sem=recv_sem.at[step],
            device_id=device(peer),
            device_id_type=MESH,
        )
        copy.start()
        sends.append(copy)
    local.wait()
    for copy in sends:
        copy.wait_send()
    for step in range(1, n):
        source = lax.rem(me + n - step, n)
        pltpu.make_async_remote_copy(
            src_ref=o_ref.at[source],
            dst_ref=o_ref.at[source],
            send_sem=send_sem.at[step],
            recv_sem=recv_sem.at[step],
            device_id=device(source),
            device_id_type=MESH,
        ).wait_recv()


def exchange(x, axis_name, gather=False):
    n = lax.axis_size(axis_name)
    key = (axis_name, gather, x.shape, str(x.dtype))
    if key not in COLLECTIVE_IDS:
        COLLECTIVE_IDS[key] = len(COLLECTIVE_IDS)
    shape = (n,) + x.shape if gather else x.shape
    return pl.pallas_call(
        functools.partial(exchange_kernel, n, axis_name, gather),
        out_shape=jax.ShapeDtypeStruct(shape, x.dtype),
        in_specs=[pl.BlockSpec(memory_space=pl.ANY)],
        out_specs=pl.BlockSpec(memory_space=pl.ANY),
        scratch_shapes=[
            pltpu.SemaphoreType.DMA((n,)),
            pltpu.SemaphoreType.DMA((n,)),
            pltpu.SemaphoreType.DMA,
        ],
        compiler_params=pltpu.CompilerParams(collective_id=COLLECTIVE_IDS[key], has_side_effects=True),
    )(x)


def onehot_sum(selected, values):
    return jnp.einsum(
        "st,tpx->spx", selected, values.astype(jnp.bfloat16), preferred_element_type=jnp.float32
    )


def a2a_gather(block, axis_name):
    size = lax.axis_size(axis_name)
    if axis_name == "cam":
        got = exchange(block, axis_name, gather=True)
    else:
        tiled = jnp.broadcast_to(block[None], (size,) + block.shape)
        got = lax.all_to_all(tiled, axis_name, 0, 0, tiled=False)
    return got.reshape((size * block.shape[0],) + block.shape[1:])


def a2a_reduce_scatter(full, axis_name):
    size = lax.axis_size(axis_name)
    chunks = full.reshape((size, full.shape[0] // size) + full.shape[1:])
    if axis_name == "cam":
        got = exchange(chunks.astype(jnp.bfloat16), axis_name)
    else:
        got = lax.all_to_all(chunks.astype(jnp.bfloat16), axis_name, 0, 0, tiled=False)
    return jnp.sum(got.astype(jnp.float32), axis=0)


def swap_kernel(x_ref, o_ref, send_sem, recv_sem, *, partner):
    barrier = pltpu.get_barrier_semaphore()
    pl.semaphore_signal(barrier, inc=1, device_id=partner(), device_id_type=MESH)
    pl.semaphore_wait(barrier, 1)
    copy = pltpu.make_async_remote_copy(
        src_ref=x_ref,
        dst_ref=o_ref,
        send_sem=send_sem,
        recv_sem=recv_sem,
        device_id=partner(),
        device_id_type=MESH,
    )
    copy.start()
    copy.wait_send()
    copy.wait_recv()


def swap(x, flip):
    key = ("swap", flip, x.shape, str(x.dtype))
    if key not in COLLECTIVE_IDS:
        COLLECTIVE_IDS[key] = len(COLLECTIVE_IDS)

    def partner():
        return (lax.axis_index("cam") ^ flip, lax.axis_index("lmk"))

    return pl.pallas_call(
        functools.partial(swap_kernel, partner=partner),
        out_shape=jax.ShapeDtypeStruct(x.shape, x.dtype),
        in_specs=[pl.BlockSpec(memory_space=pl.ANY)],
        out_specs=pl.BlockSpec(memory_space=pl.ANY),
        scratch_shapes=[pltpu.SemaphoreType.DMA, pltpu.SemaphoreType.DMA],
        compiler_params=pltpu.CompilerParams(collective_id=COLLECTIVE_IDS[key], has_side_effects=True),
    )(x)


def pick(flag, a, b):
    return jnp.where(flag == 0, a, b)


def cam_reduce(partial_value):
    chunk = partial_value.shape[0] // 4
    chip = partial_value[2 * chunk:] + swap(partial_value[: 2 * chunk].astype(jnp.bfloat16), 1).astype(jnp.float32)
    return chip[:chunk] + swap(chip[chunk:].astype(jnp.bfloat16), 2).astype(jnp.float32)


def reduce_order(landmark_count):
    cam = lax.axis_index("cam")
    core, high = cam % 2, cam // 2
    chunk = landmark_count // 4
    rows = jnp.arange(landmark_count, dtype=jnp.int32)
    group, offset = rows // chunk, rows % chunk
    chunk_core = jnp.where(group < 2, 1 - core, core)
    chunk_high = jnp.where(group % 2 == 0, high, 1 - high)
    return (chunk_high * 2 + chunk_core) * chunk + offset


def cam_gather_kernel(x_ref, o_ref, send_sem, recv_sem, local_sem):
    cam = lax.axis_index("cam")
    lmk = lax.axis_index("lmk")
    core_peer, high_peer = cam ^ 1, cam ^ 2
    barrier = pltpu.get_barrier_semaphore()
    for peer in (core_peer, high_peer):
        pl.semaphore_signal(barrier, inc=1, device_id=(peer, lmk), device_id_type=MESH)
    pl.semaphore_wait(barrier, 2)

    def remote(src, dst, slot, peer):
        return pltpu.make_async_remote_copy(
            src_ref=src,
            dst_ref=dst,
            send_sem=send_sem.at[slot],
            recv_sem=recv_sem.at[slot],
            device_id=(peer, lmk),
            device_id_type=MESH,
        )

    local = pltpu.make_async_copy(x_ref, o_ref.at[cam], local_sem)
    local.start()
    to_high = remote(x_ref, o_ref.at[cam], 0, high_peer)
    to_high.start()
    to_core = remote(x_ref, o_ref.at[cam], 1, core_peer)
    to_core.start()
    remote(o_ref.at[high_peer], o_ref.at[high_peer], 0, high_peer).wait_recv()
    relay = remote(o_ref.at[high_peer], o_ref.at[high_peer], 2, core_peer)
    relay.start()
    local.wait()
    to_high.wait_send()
    to_core.wait_send()
    relay.wait_send()
    remote(o_ref.at[core_peer], o_ref.at[core_peer], 1, core_peer).wait_recv()
    remote(o_ref.at[cam ^ 3], o_ref.at[cam ^ 3], 2, core_peer).wait_recv()


def cam_gather(block):
    key = ("cam_gather", block.shape, str(block.dtype))
    if key not in COLLECTIVE_IDS:
        COLLECTIVE_IDS[key] = len(COLLECTIVE_IDS)
    full = pl.pallas_call(
        cam_gather_kernel,
        out_shape=jax.ShapeDtypeStruct((4,) + block.shape, block.dtype),
        in_specs=[pl.BlockSpec(memory_space=pl.ANY)],
        out_specs=pl.BlockSpec(memory_space=pl.ANY),
        scratch_shapes=[
            pltpu.SemaphoreType.DMA((3,)),
            pltpu.SemaphoreType.DMA((3,)),
            pltpu.SemaphoreType.DMA,
        ],
        compiler_params=pltpu.CompilerParams(collective_id=COLLECTIVE_IDS[key], has_side_effects=True),
    )(block)
    return full.reshape((4 * block.shape[0],) + block.shape[1:])


def local(probes, u_inverse, couplings, v_inverse, tile_cam, tile_lmk):
    group_size = lax.axis_size("lmk") * u_inverse.shape[0]
    landmark_count = v_inverse.shape[0]
    cam_onehot = (tile_cam[None, :] == jnp.arange(group_size, dtype=jnp.int32)[:, None]).astype(
        jnp.bfloat16
    )
    lmk_onehot = (tile_lmk[None, :] == reduce_order(landmark_count)[:, None]).astype(
        jnp.bfloat16
    )
    cam_count = lax.axis_size("cam")
    part_size = landmark_count // cam_count
    v_part = lax.dynamic_slice_in_dim(v_inverse, lax.axis_index("cam") * part_size, part_size, 0)
    current = jnp.einsum("bpc,bcd->bpd", probes, u_inverse, preferred_element_type=jnp.float32)
    series_sum = current
    panel = a2a_gather(current.astype(jnp.bfloat16), "lmk")
    for power_step in range(POWERS):
        tile_rows = jnp.take(panel, tile_cam, axis=0)
        forward = jnp.einsum(
            "tpc,tcl->tpl", tile_rows, couplings, preferred_element_type=jnp.float32
        )
        partial_value = onehot_sum(lmk_onehot, forward)
        landmark_part = cam_reduce(partial_value)
        landmark_part_out = jnp.einsum(
            "mpl,mlq->mpq",
            landmark_part.astype(jnp.bfloat16),
            v_part,
            preferred_element_type=jnp.float32,
        ).astype(jnp.bfloat16)
        landmark_out = cam_gather(landmark_part_out)
        picked = jnp.take(landmark_out, tile_lmk, axis=0)
        backward = jnp.einsum("tpl,tcl->tpc", picked, couplings, preferred_element_type=jnp.float32)
        camera_sum = a2a_reduce_scatter(onehot_sum(cam_onehot, backward), "lmk")
        current = jnp.einsum(
            "bpc,bcd->bpd",
            camera_sum.astype(jnp.bfloat16),
            u_inverse,
            preferred_element_type=jnp.float32,
        )
        series_sum = series_sum + current
        if power_step + 1 < POWERS:
            panel = a2a_gather(current.astype(jnp.bfloat16), "lmk")
    return series_sum


def solution(mesh):
    COLLECTIVE_IDS.clear()
    in_specs = (
        P(("cam", "lmk"), None, None),
        P(("cam", "lmk"), None, None),
        P(("cam", "lmk"), None, None),
        P("lmk", None, None),
        P(("cam", "lmk")),
        P(("cam", "lmk")),
    )
    out_specs = P(("cam", "lmk"), None, None)
    return jax.shard_map(local, mesh=mesh, in_specs=in_specs, out_specs=out_specs, check_vma=False)
```

```python
import functools

import jax
import jax.numpy as jnp
from jax import lax
from jax.experimental import pallas as pl
from jax.experimental.pallas import tpu as pltpu
from jax.sharding import PartitionSpec as P

POWERS = 4
MESH = pl.DeviceIdType.MESH
AXES = ("cam", "lmk")
COLLECTIVE_IDS = {}


def exchange_kernel(n, axis, gather, x_ref, o_ref, send_sem, recv_sem, local_sem):
    me = lax.axis_index(axis)
    coords = tuple(lax.axis_index(name) for name in AXES)
    slot = AXES.index(axis)

    def device(peer):
        return coords[:slot] + (peer,) + coords[slot + 1:]

    barrier = pltpu.get_barrier_semaphore()
    for step in range(1, n):
        pl.semaphore_signal(barrier, inc=1, device_id=device(lax.rem(me + step, n)), device_id_type=MESH)
    pl.semaphore_wait(barrier, n - 1)
    local = pltpu.make_async_copy(x_ref if gather else x_ref.at[me], o_ref.at[me], local_sem)
    local.start()
    sends = []
    for step in range(1, n):
        peer = lax.rem(me + step, n)
        copy = pltpu.make_async_remote_copy(
            src_ref=x_ref if gather else x_ref.at[peer],
            dst_ref=o_ref.at[me],
            send_sem=send_sem.at[step],
            recv_sem=recv_sem.at[step],
            device_id=device(peer),
            device_id_type=MESH,
        )
        copy.start()
        sends.append(copy)
    local.wait()
    for copy in sends:
        copy.wait_send()
    for step in range(1, n):
        source = lax.rem(me + n - step, n)
        pltpu.make_async_remote_copy(
            src_ref=o_ref.at[source],
            dst_ref=o_ref.at[source],
            send_sem=send_sem.at[step],
            recv_sem=recv_sem.at[step],
            device_id=device(source),
            device_id_type=MESH,
        ).wait_recv()


def exchange(x, axis_name, gather=False):
    n = lax.axis_size(axis_name)
    key = (axis_name, gather, x.shape, str(x.dtype))
    if key not in COLLECTIVE_IDS:
        COLLECTIVE_IDS[key] = len(COLLECTIVE_IDS)
    shape = (n,) + x.shape if gather else x.shape
    return pl.pallas_call(
        functools.partial(exchange_kernel, n, axis_name, gather),
        out_shape=jax.ShapeDtypeStruct(shape, x.dtype),
        in_specs=[pl.BlockSpec(memory_space=pl.ANY)],
        out_specs=pl.BlockSpec(memory_space=pl.ANY),
        scratch_shapes=[
            pltpu.SemaphoreType.DMA((n,)),
            pltpu.SemaphoreType.DMA((n,)),
            pltpu.SemaphoreType.DMA,
        ],
        compiler_params=pltpu.CompilerParams(collective_id=COLLECTIVE_IDS[key], has_side_effects=True),
    )(x)


def onehot_sum(selected, values):
    return jnp.einsum(
        "st,tpx->spx", selected, values.astype(jnp.bfloat16), preferred_element_type=jnp.float32
    )


def a2a_gather(block, axis_name):
    size = lax.axis_size(axis_name)
    if axis_name == "cam":
        got = exchange(block, axis_name, gather=True)
    else:
        tiled = jnp.broadcast_to(block[None], (size,) + block.shape)
        got = lax.all_to_all(tiled, axis_name, 0, 0, tiled=False)
    return got.reshape((size * block.shape[0],) + block.shape[1:])


def a2a_reduce_scatter(full, axis_name):
    size = lax.axis_size(axis_name)
    chunks = full.reshape((size, full.shape[0] // size) + full.shape[1:])
    if axis_name == "cam":
        got = exchange(chunks.astype(jnp.bfloat16), axis_name)
    else:
        got = lax.all_to_all(chunks.astype(jnp.bfloat16), axis_name, 0, 0, tiled=False)
    return jnp.sum(got.astype(jnp.float32), axis=0)


def swap_kernel(x_ref, o_ref, send_sem, recv_sem, *, partner):
    barrier = pltpu.get_barrier_semaphore()
    pl.semaphore_signal(barrier, inc=1, device_id=partner(), device_id_type=MESH)
    pl.semaphore_wait(barrier, 1)
    copy = pltpu.make_async_remote_copy(
        src_ref=x_ref,
        dst_ref=o_ref,
        send_sem=send_sem,
        recv_sem=recv_sem,
        device_id=partner(),
        device_id_type=MESH,
    )
    copy.start()
    copy.wait_send()
    copy.wait_recv()


def swap(x, flip):
    key = ("swap", flip, x.shape, str(x.dtype))
    if key not in COLLECTIVE_IDS:
        COLLECTIVE_IDS[key] = len(COLLECTIVE_IDS)

    def partner():
        return (lax.axis_index("cam") ^ flip, lax.axis_index("lmk"))

    return pl.pallas_call(
        functools.partial(swap_kernel, partner=partner),
        out_shape=jax.ShapeDtypeStruct(x.shape, x.dtype),
        in_specs=[pl.BlockSpec(memory_space=pl.ANY)],
        out_specs=pl.BlockSpec(memory_space=pl.ANY),
        scratch_shapes=[pltpu.SemaphoreType.DMA, pltpu.SemaphoreType.DMA],
        compiler_params=pltpu.CompilerParams(collective_id=COLLECTIVE_IDS[key], has_side_effects=True),
    )(x)


def pick(flag, a, b):
    return jnp.where(flag == 0, a, b)


def cam_reduce(theirs, mine):
    chunk = mine.shape[0] // 2
    chip = mine + swap(theirs, 1).astype(jnp.float32)
    return chip[:chunk] + swap(chip[chunk:].astype(jnp.bfloat16), 2).astype(jnp.float32)


def reduce_order(landmark_count):
    cam = lax.axis_index("cam")
    core, high = cam % 2, cam // 2
    chunk = landmark_count // 4
    rows = jnp.arange(landmark_count, dtype=jnp.int32)
    group, offset = rows // chunk, rows % chunk
    chunk_core = jnp.where(group < 2, 1 - core, core)
    chunk_high = jnp.where(group % 2 == 0, high, 1 - high)
    return (chunk_high * 2 + chunk_core) * chunk + offset


def cam_gather_kernel(x_ref, o_ref, send_sem, recv_sem, local_sem):
    cam = lax.axis_index("cam")
    lmk = lax.axis_index("lmk")
    core_peer, high_peer = cam ^ 1, cam ^ 2
    barrier = pltpu.get_barrier_semaphore()
    for peer in (core_peer, high_peer):
        pl.semaphore_signal(barrier, inc=1, device_id=(peer, lmk), device_id_type=MESH)
    pl.semaphore_wait(barrier, 2)

    def remote(src, dst, slot, peer):
        return pltpu.make_async_remote_copy(
            src_ref=src,
            dst_ref=dst,
            send_sem=send_sem.at[slot],
            recv_sem=recv_sem.at[slot],
            device_id=(peer, lmk),
            device_id_type=MESH,
        )

    local = pltpu.make_async_copy(x_ref, o_ref.at[cam], local_sem)
    local.start()
    to_high = remote(x_ref, o_ref.at[cam], 0, high_peer)
    to_high.start()
    to_core = remote(x_ref, o_ref.at[cam], 1, core_peer)
    to_core.start()
    remote(o_ref.at[high_peer], o_ref.at[high_peer], 0, high_peer).wait_recv()
    relay = remote(o_ref.at[high_peer], o_ref.at[high_peer], 2, core_peer)
    relay.start()
    local.wait()
    to_high.wait_send()
    to_core.wait_send()
    relay.wait_send()
    remote(o_ref.at[core_peer], o_ref.at[core_peer], 1, core_peer).wait_recv()
    remote(o_ref.at[cam ^ 3], o_ref.at[cam ^ 3], 2, core_peer).wait_recv()


def cam_gather(block):
    key = ("cam_gather", block.shape, str(block.dtype))
    if key not in COLLECTIVE_IDS:
        COLLECTIVE_IDS[key] = len(COLLECTIVE_IDS)
    full = pl.pallas_call(
        cam_gather_kernel,
        out_shape=jax.ShapeDtypeStruct((4,) + block.shape, block.dtype),
        in_specs=[pl.BlockSpec(memory_space=pl.ANY)],
        out_specs=pl.BlockSpec(memory_space=pl.ANY),
        scratch_shapes=[
            pltpu.SemaphoreType.DMA((3,)),
            pltpu.SemaphoreType.DMA((3,)),
            pltpu.SemaphoreType.DMA,
        ],
        compiler_params=pltpu.CompilerParams(collective_id=COLLECTIVE_IDS[key], has_side_effects=True),
    )(block)
    return full.reshape((4 * block.shape[0],) + block.shape[1:])


def local(probes, u_inverse, couplings, v_inverse, tile_cam, tile_lmk):
    group_size = lax.axis_size("lmk") * u_inverse.shape[0]
    landmark_count = v_inverse.shape[0]
    cam_onehot = (tile_cam[None, :] == jnp.arange(group_size, dtype=jnp.int32)[:, None]).astype(
        jnp.bfloat16
    )
    lmk_onehot = (tile_lmk[None, :] == reduce_order(landmark_count)[:, None]).astype(
        jnp.bfloat16
    )
    cam_count = lax.axis_size("cam")
    part_size = landmark_count // cam_count
    v_part = lax.dynamic_slice_in_dim(v_inverse, lax.axis_index("cam") * part_size, part_size, 0)
    current = jnp.einsum("bpc,bcd->bpd", probes, u_inverse, preferred_element_type=jnp.float32)
    series_sum = current
    panel = a2a_gather(current.astype(jnp.bfloat16), "lmk")
    for power_step in range(POWERS):
        tile_rows = jnp.take(panel, tile_cam, axis=0)
        forward = jnp.einsum(
            "tpc,tcl->tpl", tile_rows, couplings, preferred_element_type=jnp.float32
        )
        forward_bf16 = forward.astype(jnp.bfloat16)
        half = lmk_onehot.shape[0] // 2
        theirs = jnp.einsum(
            "st,tpx->spx", lmk_onehot[:half], forward_bf16, preferred_element_type=jnp.float32
        ).astype(jnp.bfloat16)
        mine = jnp.einsum(
            "st,tpx->spx", lmk_onehot[half:], forward_bf16, preferred_element_type=jnp.float32
        )
        landmark_part = cam_reduce(theirs, mine)
        landmark_part_out = jnp.einsum(
            "mpl,mlq->mpq",
            landmark_part.astype(jnp.bfloat16),
            v_part,
            preferred_element_type=jnp.float32,
        ).astype(jnp.bfloat16)
        landmark_out = cam_gather(landmark_part_out)
        picked = jnp.take(landmark_out, tile_lmk, axis=0)
        backward = jnp.einsum("tpl,tcl->tpc", picked, couplings, preferred_element_type=jnp.float32)
        camera_sum = a2a_reduce_scatter(onehot_sum(cam_onehot, backward), "lmk")
        current = jnp.einsum(
            "bpc,bcd->bpd",
            camera_sum.astype(jnp.bfloat16),
            u_inverse,
            preferred_element_type=jnp.float32,
        )
        series_sum = series_sum + current
        if power_step + 1 < POWERS:
            panel = a2a_gather(current.astype(jnp.bfloat16), "lmk")
    return series_sum


def solution(mesh):
    COLLECTIVE_IDS.clear()
    in_specs = (
        P(("cam", "lmk"), None, None),
        P(("cam", "lmk"), None, None),
        P(("cam", "lmk"), None, None),
        P("lmk", None, None),
        P(("cam", "lmk")),
        P(("cam", "lmk")),
    )
    out_specs = P(("cam", "lmk"), None, None)
    return jax.shard_map(local, mesh=mesh, in_specs=in_specs, out_specs=out_specs, check_vma=False)
```

```python
import functools

import jax
import jax.numpy as jnp
from jax import lax
from jax.experimental import pallas as pl
from jax.experimental.pallas import tpu as pltpu
from jax.sharding import PartitionSpec as P

POWERS = 4
MESH = pl.DeviceIdType.MESH
AXES = ("cam", "lmk")
COLLECTIVE_IDS = {}


def exchange_kernel(n, axis, gather, x_ref, o_ref, send_sem, recv_sem, local_sem):
    me = lax.axis_index(axis)
    coords = tuple(lax.axis_index(name) for name in AXES)
    slot = AXES.index(axis)

    def device(peer):
        return coords[:slot] + (peer,) + coords[slot + 1:]

    barrier = pltpu.get_barrier_semaphore()
    for step in range(1, n):
        pl.semaphore_signal(barrier, inc=1, device_id=device(lax.rem(me + step, n)), device_id_type=MESH)
    pl.semaphore_wait(barrier, n - 1)
    local = pltpu.make_async_copy(x_ref if gather else x_ref.at[me], o_ref.at[me], local_sem)
    local.start()
    sends = []
    for step in range(1, n):
        peer = lax.rem(me + step, n)
        copy = pltpu.make_async_remote_copy(
            src_ref=x_ref if gather else x_ref.at[peer],
            dst_ref=o_ref.at[me],
            send_sem=send_sem.at[step],
            recv_sem=recv_sem.at[step],
            device_id=device(peer),
            device_id_type=MESH,
        )
        copy.start()
        sends.append(copy)
    local.wait()
    for copy in sends:
        copy.wait_send()
    for step in range(1, n):
        source = lax.rem(me + n - step, n)
        pltpu.make_async_remote_copy(
            src_ref=o_ref.at[source],
            dst_ref=o_ref.at[source],
            send_sem=send_sem.at[step],
            recv_sem=recv_sem.at[step],
            device_id=device(source),
            device_id_type=MESH,
        ).wait_recv()


def exchange(x, axis_name, gather=False):
    n = lax.axis_size(axis_name)
    key = (axis_name, gather, x.shape, str(x.dtype))
    if key not in COLLECTIVE_IDS:
        COLLECTIVE_IDS[key] = len(COLLECTIVE_IDS)
    shape = (n,) + x.shape if gather else x.shape
    return pl.pallas_call(
        functools.partial(exchange_kernel, n, axis_name, gather),
        out_shape=jax.ShapeDtypeStruct(shape, x.dtype),
        in_specs=[pl.BlockSpec(memory_space=pl.ANY)],
        out_specs=pl.BlockSpec(memory_space=pl.ANY),
        scratch_shapes=[
            pltpu.SemaphoreType.DMA((n,)),
            pltpu.SemaphoreType.DMA((n,)),
            pltpu.SemaphoreType.DMA,
        ],
        compiler_params=pltpu.CompilerParams(collective_id=COLLECTIVE_IDS[key], has_side_effects=True),
    )(x)


def onehot_sum(selected, values):
    return jnp.einsum(
        "st,tpx->spx", selected, values.astype(jnp.bfloat16), preferred_element_type=jnp.float32
    )


def a2a_gather(block, axis_name):
    size = lax.axis_size(axis_name)
    if axis_name == "cam":
        got = exchange(block, axis_name, gather=True)
    else:
        tiled = jnp.broadcast_to(block[None], (size,) + block.shape)
        got = lax.all_to_all(tiled, axis_name, 0, 0, tiled=False)
    return got.reshape((size * block.shape[0],) + block.shape[1:])


def a2a_reduce_scatter(full, axis_name):
    size = lax.axis_size(axis_name)
    chunks = full.reshape((size, full.shape[0] // size) + full.shape[1:])
    if axis_name == "cam":
        got = exchange(chunks.astype(jnp.bfloat16), axis_name)
    else:
        got = lax.all_to_all(chunks.astype(jnp.bfloat16), axis_name, 0, 0, tiled=False)
    return jnp.sum(got.astype(jnp.float32), axis=0)


def swap_kernel(x_ref, o_ref, send_sem, recv_sem, *, partner):
    barrier = pltpu.get_barrier_semaphore()
    pl.semaphore_signal(barrier, inc=1, device_id=partner(), device_id_type=MESH)
    pl.semaphore_wait(barrier, 1)
    copy = pltpu.make_async_remote_copy(
        src_ref=x_ref,
        dst_ref=o_ref,
        send_sem=send_sem,
        recv_sem=recv_sem,
        device_id=partner(),
        device_id_type=MESH,
    )
    copy.start()
    copy.wait_send()
    copy.wait_recv()


def swap(x, flip):
    key = ("swap", flip, x.shape, str(x.dtype))
    if key not in COLLECTIVE_IDS:
        COLLECTIVE_IDS[key] = len(COLLECTIVE_IDS)

    def partner():
        return (lax.axis_index("cam") ^ flip, lax.axis_index("lmk"))

    return pl.pallas_call(
        functools.partial(swap_kernel, partner=partner),
        out_shape=jax.ShapeDtypeStruct(x.shape, x.dtype),
        in_specs=[pl.BlockSpec(memory_space=pl.ANY)],
        out_specs=pl.BlockSpec(memory_space=pl.ANY),
        scratch_shapes=[pltpu.SemaphoreType.DMA, pltpu.SemaphoreType.DMA],
        compiler_params=pltpu.CompilerParams(collective_id=COLLECTIVE_IDS[key], has_side_effects=True),
    )(x)


def pick(flag, a, b):
    return jnp.where(flag == 0, a, b)


def cam_reduce(partial_value):
    chunk = partial_value.shape[0] // 4
    chip = partial_value[2 * chunk:] + swap(partial_value[: 2 * chunk].astype(jnp.bfloat16), 1).astype(jnp.float32)
    return chip[:chunk] + swap(chip[chunk:].astype(jnp.bfloat16), 2).astype(jnp.float32)


def reduce_order(landmark_count):
    cam = lax.axis_index("cam")
    core, high = cam % 2, cam // 2
    chunk = landmark_count // 4
    rows = jnp.arange(landmark_count, dtype=jnp.int32)
    group, offset = rows // chunk, rows % chunk
    chunk_core = jnp.where(group < 2, 1 - core, core)
    chunk_high = jnp.where(group % 2 == 0, high, 1 - high)
    return (chunk_high * 2 + chunk_core) * chunk + offset


def cam_gather_kernel(x_ref, o_ref, send_sem, recv_sem, local_sem):
    cam = lax.axis_index("cam")
    lmk = lax.axis_index("lmk")
    core_peer, high_peer = cam ^ 1, cam ^ 2
    barrier = pltpu.get_barrier_semaphore()
    for peer in (core_peer, high_peer):
        pl.semaphore_signal(barrier, inc=1, device_id=(peer, lmk), device_id_type=MESH)
    pl.semaphore_wait(barrier, 2)

    def remote(src, dst, slot, peer):
        return pltpu.make_async_remote_copy(
            src_ref=src,
            dst_ref=dst,
            send_sem=send_sem.at[slot],
            recv_sem=recv_sem.at[slot],
            device_id=(peer, lmk),
            device_id_type=MESH,
        )

    local = pltpu.make_async_copy(x_ref, o_ref.at[cam], local_sem)
    local.start()
    to_high = remote(x_ref, o_ref.at[cam], 0, high_peer)
    to_high.start()
    to_core = remote(x_ref, o_ref.at[cam], 1, core_peer)
    to_core.start()
    remote(o_ref.at[high_peer], o_ref.at[high_peer], 0, high_peer).wait_recv()
    relay = remote(o_ref.at[high_peer], o_ref.at[high_peer], 2, core_peer)
    relay.start()
    local.wait()
    to_high.wait_send()
    to_core.wait_send()
    relay.wait_send()
    remote(o_ref.at[core_peer], o_ref.at[core_peer], 1, core_peer).wait_recv()
    remote(o_ref.at[cam ^ 3], o_ref.at[cam ^ 3], 2, core_peer).wait_recv()


def cam_gather(block):
    key = ("cam_gather", block.shape, str(block.dtype))
    if key not in COLLECTIVE_IDS:
        COLLECTIVE_IDS[key] = len(COLLECTIVE_IDS)
    full = pl.pallas_call(
        cam_gather_kernel,
        out_shape=jax.ShapeDtypeStruct((4,) + block.shape, block.dtype),
        in_specs=[pl.BlockSpec(memory_space=pl.ANY)],
        out_specs=pl.BlockSpec(memory_space=pl.ANY),
        scratch_shapes=[
            pltpu.SemaphoreType.DMA((3,)),
            pltpu.SemaphoreType.DMA((3,)),
            pltpu.SemaphoreType.DMA,
        ],
        compiler_params=pltpu.CompilerParams(collective_id=COLLECTIVE_IDS[key], has_side_effects=True),
    )(block)
    return full.reshape((4 * block.shape[0],) + block.shape[1:])


def local(probes, u_inverse, couplings, v_inverse, tile_cam, tile_lmk):
    group_size = lax.axis_size("lmk") * u_inverse.shape[0]
    landmark_count = v_inverse.shape[0]
    cam_onehot = (tile_cam[None, :] == jnp.arange(group_size, dtype=jnp.int32)[:, None]).astype(
        jnp.bfloat16
    )
    lmk_onehot = (tile_lmk[None, :] == reduce_order(landmark_count)[:, None]).astype(
        jnp.bfloat16
    )
    cam_count = lax.axis_size("cam")
    part_size = landmark_count // cam_count
    v_part = lax.dynamic_slice_in_dim(v_inverse, lax.axis_index("cam") * part_size, part_size, 0)
    current = jnp.einsum("bpc,bcd->bpd", probes, u_inverse, preferred_element_type=jnp.float32)
    series_sum = current
    panel = a2a_gather(current.astype(jnp.bfloat16), "lmk")
    for power_step in range(POWERS):
        tile_rows = jnp.take(panel.reshape(panel.shape[0], -1), tile_cam, axis=0).reshape(
            tile_cam.shape + panel.shape[1:]
        )
        forward = jnp.einsum(
            "tpc,tcl->tpl", tile_rows, couplings, preferred_element_type=jnp.float32
        )
        partial_value = onehot_sum(lmk_onehot, forward)
        landmark_part = cam_reduce(partial_value)
        landmark_part_out = jnp.einsum(
            "mpl,mlq->mpq",
            landmark_part.astype(jnp.bfloat16),
            v_part,
            preferred_element_type=jnp.float32,
        ).astype(jnp.bfloat16)
        landmark_out = cam_gather(landmark_part_out)
        picked = jnp.take(landmark_out, tile_lmk, axis=0)
        backward = jnp.einsum("tpl,tcl->tpc", picked, couplings, preferred_element_type=jnp.float32)
        camera_sum = a2a_reduce_scatter(onehot_sum(cam_onehot, backward), "lmk")
        current = jnp.einsum(
            "bpc,bcd->bpd",
            camera_sum.astype(jnp.bfloat16),
            u_inverse,
            preferred_element_type=jnp.float32,
        )
        series_sum = series_sum + current
        if power_step + 1 < POWERS:
            panel = a2a_gather(current.astype(jnp.bfloat16), "lmk")
    return series_sum


def solution(mesh):
    COLLECTIVE_IDS.clear()
    in_specs = (
        P(("cam", "lmk"), None, None),
        P(("cam", "lmk"), None, None),
        P(("cam", "lmk"), None, None),
        P("lmk", None, None),
        P(("cam", "lmk")),
        P(("cam", "lmk")),
    )
    out_specs = P(("cam", "lmk"), None, None)
    return jax.shard_map(local, mesh=mesh, in_specs=in_specs, out_specs=out_specs, check_vma=False)
```

```python
import functools

import jax
import jax.numpy as jnp
from jax import lax
from jax.experimental import pallas as pl
from jax.experimental.pallas import tpu as pltpu
from jax.sharding import PartitionSpec as P

POWERS = 4
MESH = pl.DeviceIdType.MESH
AXES = ("cam", "lmk")
COLLECTIVE_IDS = {}


def exchange_kernel(n, axis, gather, x_ref, o_ref, send_sem, recv_sem, local_sem):
    me = lax.axis_index(axis)
    coords = tuple(lax.axis_index(name) for name in AXES)
    slot = AXES.index(axis)

    def device(peer):
        return coords[:slot] + (peer,) + coords[slot + 1:]

    barrier = pltpu.get_barrier_semaphore()
    for step in range(1, n):
        pl.semaphore_signal(barrier, inc=1, device_id=device(lax.rem(me + step, n)), device_id_type=MESH)
    pl.semaphore_wait(barrier, n - 1)
    local = pltpu.make_async_copy(x_ref if gather else x_ref.at[me], o_ref.at[me], local_sem)
    local.start()
    sends = []
    for step in range(1, n):
        peer = lax.rem(me + step, n)
        copy = pltpu.make_async_remote_copy(
            src_ref=x_ref if gather else x_ref.at[peer],
            dst_ref=o_ref.at[me],
            send_sem=send_sem.at[step],
            recv_sem=recv_sem.at[step],
            device_id=device(peer),
            device_id_type=MESH,
        )
        copy.start()
        sends.append(copy)
    local.wait()
    for copy in sends:
        copy.wait_send()
    for step in range(1, n):
        source = lax.rem(me + n - step, n)
        pltpu.make_async_remote_copy(
            src_ref=o_ref.at[source],
            dst_ref=o_ref.at[source],
            send_sem=send_sem.at[step],
            recv_sem=recv_sem.at[step],
            device_id=device(source),
            device_id_type=MESH,
        ).wait_recv()


def exchange(x, axis_name, gather=False):
    n = lax.axis_size(axis_name)
    key = (axis_name, gather, x.shape, str(x.dtype))
    if key not in COLLECTIVE_IDS:
        COLLECTIVE_IDS[key] = len(COLLECTIVE_IDS)
    shape = (n,) + x.shape if gather else x.shape
    return pl.pallas_call(
        functools.partial(exchange_kernel, n, axis_name, gather),
        out_shape=jax.ShapeDtypeStruct(shape, x.dtype),
        in_specs=[pl.BlockSpec(memory_space=pl.ANY)],
        out_specs=pl.BlockSpec(memory_space=pl.ANY),
        scratch_shapes=[
            pltpu.SemaphoreType.DMA((n,)),
            pltpu.SemaphoreType.DMA((n,)),
            pltpu.SemaphoreType.DMA,
        ],
        compiler_params=pltpu.CompilerParams(collective_id=COLLECTIVE_IDS[key], has_side_effects=True),
    )(x)


def onehot_sum(selected, values):
    return jnp.einsum(
        "st,tpx->spx", selected, values.astype(jnp.bfloat16), preferred_element_type=jnp.float32
    )


def a2a_gather(block, axis_name):
    size = lax.axis_size(axis_name)
    if axis_name == "cam":
        got = exchange(block, axis_name, gather=True)
    else:
        tiled = jnp.broadcast_to(block[None], (size,) + block.shape)
        got = lax.all_to_all(tiled, axis_name, 0, 0, tiled=False)
    return got.reshape((size * block.shape[0],) + block.shape[1:])


def a2a_reduce_scatter(full, axis_name):
    size = lax.axis_size(axis_name)
    chunks = full.reshape((size, full.shape[0] // size) + full.shape[1:])
    if axis_name == "cam":
        got = exchange(chunks.astype(jnp.bfloat16), axis_name)
    else:
        if full.shape[0] == size:
            got = lax.all_to_all(full.astype(jnp.bfloat16), axis_name, 0, 0, tiled=True)
            return jnp.sum(got.astype(jnp.float32), axis=0, keepdims=True)
        got = lax.all_to_all(chunks.astype(jnp.bfloat16), axis_name, 0, 0, tiled=False)
    return jnp.sum(got.astype(jnp.float32), axis=0)


def swap_kernel(x_ref, o_ref, send_sem, recv_sem, *, partner):
    barrier = pltpu.get_barrier_semaphore()
    pl.semaphore_signal(barrier, inc=1, device_id=partner(), device_id_type=MESH)
    pl.semaphore_wait(barrier, 1)
    copy = pltpu.make_async_remote_copy(
        src_ref=x_ref,
        dst_ref=o_ref,
        send_sem=send_sem,
        recv_sem=recv_sem,
        device_id=partner(),
        device_id_type=MESH,
    )
    copy.start()
    copy.wait_send()
    copy.wait_recv()


def swap(x, flip):
    key = ("swap", flip, x.shape, str(x.dtype))
    if key not in COLLECTIVE_IDS:
        COLLECTIVE_IDS[key] = len(COLLECTIVE_IDS)

    def partner():
        return (lax.axis_index("cam") ^ flip, lax.axis_index("lmk"))

    return pl.pallas_call(
        functools.partial(swap_kernel, partner=partner),
        out_shape=jax.ShapeDtypeStruct(x.shape, x.dtype),
        in_specs=[pl.BlockSpec(memory_space=pl.ANY)],
        out_specs=pl.BlockSpec(memory_space=pl.ANY),
        scratch_shapes=[pltpu.SemaphoreType.DMA, pltpu.SemaphoreType.DMA],
        compiler_params=pltpu.CompilerParams(collective_id=COLLECTIVE_IDS[key], has_side_effects=True),
    )(x)


def pick(flag, a, b):
    return jnp.where(flag == 0, a, b)


def cam_reduce(partial_value):
    chunk = partial_value.shape[0] // 4
    chip = partial_value[2 * chunk:] + swap(partial_value[: 2 * chunk].astype(jnp.bfloat16), 1).astype(jnp.float32)
    return chip[:chunk] + swap(chip[chunk:].astype(jnp.bfloat16), 2).astype(jnp.float32)


def reduce_order(landmark_count):
    cam = lax.axis_index("cam")
    core, high = cam % 2, cam // 2
    chunk = landmark_count // 4
    rows = jnp.arange(landmark_count, dtype=jnp.int32)
    group, offset = rows // chunk, rows % chunk
    chunk_core = jnp.where(group < 2, 1 - core, core)
    chunk_high = jnp.where(group % 2 == 0, high, 1 - high)
    return (chunk_high * 2 + chunk_core) * chunk + offset


def cam_gather_kernel(x_ref, o_ref, send_sem, recv_sem, local_sem):
    cam = lax.axis_index("cam")
    lmk = lax.axis_index("lmk")
    core_peer, high_peer = cam ^ 1, cam ^ 2
    barrier = pltpu.get_barrier_semaphore()
    for peer in (core_peer, high_peer):
        pl.semaphore_signal(barrier, inc=1, device_id=(peer, lmk), device_id_type=MESH)
    pl.semaphore_wait(barrier, 2)

    def remote(src, dst, slot, peer):
        return pltpu.make_async_remote_copy(
            src_ref=src,
            dst_ref=dst,
            send_sem=send_sem.at[slot],
            recv_sem=recv_sem.at[slot],
            device_id=(peer, lmk),
            device_id_type=MESH,
        )

    local = pltpu.make_async_copy(x_ref, o_ref.at[cam], local_sem)
    local.start()
    to_high = remote(x_ref, o_ref.at[cam], 0, high_peer)
    to_high.start()
    to_core = remote(x_ref, o_ref.at[cam], 1, core_peer)
    to_core.start()
    remote(o_ref.at[high_peer], o_ref.at[high_peer], 0, high_peer).wait_recv()
    relay = remote(o_ref.at[high_peer], o_ref.at[high_peer], 2, core_peer)
    relay.start()
    local.wait()
    to_high.wait_send()
    to_core.wait_send()
    relay.wait_send()
    remote(o_ref.at[core_peer], o_ref.at[core_peer], 1, core_peer).wait_recv()
    remote(o_ref.at[cam ^ 3], o_ref.at[cam ^ 3], 2, core_peer).wait_recv()


def cam_gather(block):
    key = ("cam_gather", block.shape, str(block.dtype))
    if key not in COLLECTIVE_IDS:
        COLLECTIVE_IDS[key] = len(COLLECTIVE_IDS)
    full = pl.pallas_call(
        cam_gather_kernel,
        out_shape=jax.ShapeDtypeStruct((4,) + block.shape, block.dtype),
        in_specs=[pl.BlockSpec(memory_space=pl.ANY)],
        out_specs=pl.BlockSpec(memory_space=pl.ANY),
        scratch_shapes=[
            pltpu.SemaphoreType.DMA((3,)),
            pltpu.SemaphoreType.DMA((3,)),
            pltpu.SemaphoreType.DMA,
        ],
        compiler_params=pltpu.CompilerParams(collective_id=COLLECTIVE_IDS[key], has_side_effects=True),
    )(block)
    return full.reshape((4 * block.shape[0],) + block.shape[1:])


def local(probes, u_inverse, couplings, v_inverse, tile_cam, tile_lmk):
    group_size = lax.axis_size("lmk") * u_inverse.shape[0]
    landmark_count = v_inverse.shape[0]
    cam_onehot = (tile_cam[None, :] == jnp.arange(group_size, dtype=jnp.int32)[:, None]).astype(
        jnp.bfloat16
    )
    lmk_onehot = (tile_lmk[None, :] == reduce_order(landmark_count)[:, None]).astype(
        jnp.bfloat16
    )
    cam_count = lax.axis_size("cam")
    part_size = landmark_count // cam_count
    v_part = lax.dynamic_slice_in_dim(v_inverse, lax.axis_index("cam") * part_size, part_size, 0)
    current = jnp.einsum("bpc,bcd->bpd", probes, u_inverse, preferred_element_type=jnp.float32)
    series_sum = current
    panel = a2a_gather(current.astype(jnp.bfloat16), "lmk")
    for power_step in range(POWERS):
        tile_rows = jnp.take(panel, tile_cam, axis=0)
        forward = jnp.einsum(
            "tpc,tcl->tpl", tile_rows, couplings, preferred_element_type=jnp.float32
        )
        partial_value = onehot_sum(lmk_onehot, forward)
        landmark_part = cam_reduce(partial_value)
        landmark_part_out = jnp.einsum(
            "mpl,mlq->mpq",
            landmark_part.astype(jnp.bfloat16),
            v_part,
            preferred_element_type=jnp.float32,
        ).astype(jnp.bfloat16)
        landmark_out = cam_gather(landmark_part_out)
        picked = jnp.take(landmark_out, tile_lmk, axis=0)
        backward = jnp.einsum("tpl,tcl->tpc", picked, couplings, preferred_element_type=jnp.float32)
        camera_sum = a2a_reduce_scatter(onehot_sum(cam_onehot, backward), "lmk")
        current = jnp.einsum(
            "bpc,bcd->bpd",
            camera_sum.astype(jnp.bfloat16),
            u_inverse,
            preferred_element_type=jnp.float32,
        )
        series_sum = series_sum + current
        if power_step + 1 < POWERS:
            panel = a2a_gather(current.astype(jnp.bfloat16), "lmk")
    return series_sum


def solution(mesh):
    COLLECTIVE_IDS.clear()
    in_specs = (
        P(("cam", "lmk"), None, None),
        P(("cam", "lmk"), None, None),
        P(("cam", "lmk"), None, None),
        P("lmk", None, None),
        P(("cam", "lmk")),
        P(("cam", "lmk")),
    )
    out_specs = P(("cam", "lmk"), None, None)
    return jax.shard_map(local, mesh=mesh, in_specs=in_specs, out_specs=out_specs, check_vma=False)
```
